32 devices in a mesh: rep: 4 (over x, core), grp: 8 (over z, y).
Axes of the slice: x: 2, y: 2, z: 4, core: 2. Of those that a mesh axis runs over, the one named last changes fastest.
Arguments:
- tokens: bfloat16 [8192, 1024], P(('rep', 'grp')), may hold values from -6 to 6
- cotangent: bfloat16 [8192, 1024], P(('rep', 'grp')), may hold values from -6 to 6
- segments: int32 [8192], P(('rep', 'grp')), may hold values from 0 to 11, as said below
- params: float32 [6602752], P('grp'), may hold values from -7 to 3
- first_moment: float32 [6602752], P('grp'), may hold values from -0.15625 to 0.15625
- second_moment: float32 [6602752], P('grp'), may hold values from 1e-06 to 0.0001
Outputs:
- activations: bfloat16 [8192, 1024], P(('rep', 'grp'))
- input_grad: float32 [8192, 1024], P(('rep', 'grp'))
- grads: float32 [6602752], P('grp')
- new_params: float32 [6602752], P('grp')
- new_first: float32 [6602752], P('grp')
- new_second: float32 [6602752], P('grp')
The draws below stay inside these ranges and needn't reach their ends.
Inputs may be any that keep to these rules, and one draw needn't show every extreme that they name: Segment numbers never fall, begin at 0 and rise by one where a segment begins. Every packed sequence of 2048 tokens holds exactly three segments: one begins at its first token, one at a position in [1, 1024) and one at a position in [1024, 2048) of the sequence.
All inputs are finite; a program needn't handle non-finite values.
Results may differ from the reference program's by a relative error of at most 0.007.
The reference program's roundings to bfloat16 on the way count: a program that leaves them out, or rounds other values in their place, can miss the bound.
Values may be sent and summed in bfloat16 or wider, within the bound.
No kernel may reach another device: no remote copies, remote signals or barrier semaphores. Data moves between devices by JAX's collectives and lax.ppermute only.
A program may use at most 256 MiB of HBM per device.

```python
import math
import jax
import jax.numpy as jnp
from jax import lax

D = 1024
INNER = 2048
HEADS = 32
HEAD_DIM = 64
STATE = 128
CONV_WIDTH = 4
STRETCH = 256
SEQ_LEN = 2048
ADAM_STEP = 3
E_IN = 4384
CONV_CH = 2304
P_RAW = 6601056
P_TOTAL = 6602752
TOKENS = 8192


def draw_params(key, part):
    total_len = P_TOTAL
    position = jnp.arange(total_len)
    noise_draw = jnp.clip(jax.random.normal(key, (total_len,), jnp.float32), -6.0, 6.0)
    spread = jax.random.uniform(jax.random.fold_in(key, 7), (total_len,), jnp.float32)
    sizes_list = [D * E_IN, INNER * D, CONV_WIDTH * CONV_CH, CONV_CH, D, INNER, HEADS, HEADS, HEADS]
    bounds = []
    running = 0
    for entries in sizes_list:
        running = running + entries
        bounds.append(running)
    region = jnp.zeros((total_len,), jnp.int32)
    for limit in bounds:
        region = region + (position >= limit).astype(jnp.int32)
    choices_list = [noise_draw * D ** (-0.5), noise_draw * INNER ** (-0.5), noise_draw * 0.5, noise_draw * 0.3, 1.0 + 0.1 * noise_draw, 1.0 + 0.1 * noise_draw, -7.0 + 4.7 * spread, -4.6 + 5.6 * spread, 0.5 + spread, noise_draw * 0.02]
    result = jnp.zeros((total_len,), jnp.float32)
    for region_id in range(len(choices_list)):
        result = jnp.where(region == region_id, choices_list[region_id], result)
    return result.astype(jnp.float32)


def draw_segments(key, part):
    seq_count = TOKENS // SEQ_LEN
    half_len = SEQ_LEN // 2
    first_cut = jax.random.randint(jax.random.fold_in(key, 11), (seq_count,), 1, half_len)
    second_cut = jax.random.randint(jax.random.fold_in(key, 12), (seq_count,), half_len, SEQ_LEN)
    within = jnp.arange(SEQ_LEN, dtype=jnp.int32)[None, :]
    level = (within >= first_cut[:, None]).astype(jnp.int32) + (within >= second_cut[:, None]).astype(jnp.int32)
    base_ids = 3 * jnp.arange(seq_count, dtype=jnp.int32)[:, None]
    return (base_ids + level).reshape(TOKENS).astype(jnp.int32)


def block_levels(rng, shape, shards, low, largest):
    def one(dim, blocks):
        draws = jax.random.uniform(jax.random.fold_in(jax.random.fold_in(rng, 6), dim), (blocks,), jnp.float32, low / len(shards), largest / len(shards))
        return jnp.repeat(jnp.exp(draws), shape[dim] // blocks).reshape((-1,) + (1,) * (len(shape) - dim - 1))

    gain = one(*shards[0])
    for cut in shards[1:]:
        gain = gain * one(*cut)
    return gain


def normal_values(stream_key, extent, scale, most, cuts=(), kind=jnp.bfloat16):
    level = block_levels(stream_key, extent, cuts, -0.22, 0.18) if cuts else 1.0
    values = jax.random.normal(stream_key, extent, jnp.float32) * scale * level
    return jnp.minimum(jnp.maximum(values, -most), most).astype(kind)


def setup_inputs(seed: int = 0) -> dict:
    key_list = jax.random.split(jax.random.key(seed), 7)
    tokens = normal_values(key_list[0], (TOKENS, D), 1.0, 6.0, ((0, 32),))
    cotangent = normal_values(key_list[1], (TOKENS, D), 1.0, 6.0, ((0, 32),))
    segments = draw_segments(jax.random.fold_in(key_list[6], 71), 0)
    params = draw_params(jax.random.fold_in(key_list[6], 71), 0)
    first_moment = normal_values(key_list[4], (P_TOTAL,), 0.01, 0.15625, ((0, 8),), jnp.float32)
    second_moment = jnp.clip(jnp.exp(math.log(0.0001) - 4.6051702 * jax.random.uniform(key_list[5], (P_TOTAL,), jnp.float32) ** block_levels(key_list[5], (P_TOTAL,), ((0, 8),), -0.2, 0.2)), 9.999999974752427e-07, 0.0001)
    return {"tokens": tokens, "cotangent": cotangent, "segments": segments, "params": params, "first_moment": first_moment, "second_moment": second_moment}


EPSILON = 1e-05
BETA_ONE = 0.9
BETA_TWO = 0.95
LEARN_RATE = 0.003
DECAY_RATE = 0.1
ADAM_EPS = 1e-08
HIGHEST = lax.Precision.HIGHEST

def param_shapes():
    return [(D, E_IN), (INNER, D), (CONV_WIDTH, CONV_CH), (CONV_CH,), (D,), (INNER,), (HEADS,), (HEADS,), (HEADS,)]

def unpack(flat):
    pieces = []
    offset = 0
    for block_shape in param_shapes():
        entries = math.prod(block_shape)
        pieces.append(flat[offset:offset + entries].reshape(block_shape))
        offset = offset + entries
    return pieces

def conv_silu(extended, ext_seg, conv_weight, conv_bias):
    length = extended.shape[0] - (CONV_WIDTH - 1)
    own_seg = ext_seg[CONV_WIDTH - 1:]
    summed = jnp.zeros((length, extended.shape[1]), jnp.float32) + conv_bias
    for kernel_tap in range(CONV_WIDTH):
        same_doc = (ext_seg[kernel_tap:kernel_tap + length] == own_seg).astype(jnp.float32)
        summed = summed + conv_weight[kernel_tap] * extended[kernel_tap:kernel_tap + length] * same_doc[:, None]
    return jax.nn.silu(summed)

def block_step(carry_in, inputs):
    carry_state, prev_seg = carry_in
    values, writes, readout, deltas, decays, seg_ids = inputs
    cumulative = jnp.cumsum(decays, axis=0)
    earlier_ids = jnp.concatenate([prev_seg[None], seg_ids[:-1]])
    starts = (seg_ids != earlier_ids).astype(jnp.int32)
    linked = (jnp.cumsum(starts) == 0).astype(jnp.float32)
    span_len = seg_ids.shape[0]
    rows_idx = lax.broadcasted_iota(jnp.int32, (span_len, span_len), 0)
    cols_idx = lax.broadcasted_iota(jnp.int32, (span_len, span_len), 1)
    allowed = ((seg_ids[:, None] == seg_ids[None, :]) & (cols_idx <= rows_idx)).astype(jnp.float32)
    gap_log = cumulative[:, None, :] - cumulative[None, :, :]
    kernel = jnp.exp(gap_log * allowed[:, :, None]) * allowed[:, :, None]
    scores = jnp.dot(readout, writes.T, precision=HIGHEST)
    mixing = kernel * scores[:, :, None]
    scaled = values * deltas[:, :, None]
    output = jnp.einsum('tsh,shp->thp', mixing, scaled, precision=HIGHEST)
    carried = jnp.einsum('tn,hpn->thp', readout, carry_state, precision=HIGHEST)
    output = output + (linked[:, None] * jnp.exp(cumulative))[:, :, None] * carried
    to_end = (seg_ids == seg_ids[-1]).astype(jnp.float32)
    end_weight = jnp.exp(cumulative[-1][None, :] - cumulative) * to_end[:, None] * deltas
    fresh_state = jnp.einsum('sh,shp,sn->hpn', end_weight, values, writes, precision=HIGHEST)
    new_state = (jnp.exp(cumulative[-1]) * linked[-1])[:, None, None] * carry_state + fresh_state
    return ((new_state, seg_ids[-1]), output)

def blocks_of(array_in, span_count):
    return array_in.reshape((span_count, STRETCH) + array_in.shape[1:])

def ssd_scan(values, writes, readout, deltas, decays, seg_ids, prev_seg, carry_state):
    span_count = values.shape[0] // STRETCH
    inputs = tuple((blocks_of(array_in, span_count) for array_in in (values, writes, readout, deltas, decays, seg_ids)))
    (final_state, last_seg), outputs = lax.scan(block_step, (carry_state, prev_seg), inputs)
    return (outputs.reshape(values.shape), final_state)

def mixer_inputs(extended, ext_seg, dt_raw, conv_weight, conv_bias, dt_bias, a_log):
    conv_out = conv_silu(extended, ext_seg, conv_weight, conv_bias)
    length = conv_out.shape[0]
    values = conv_out[:, :INNER].reshape(length, HEADS, HEAD_DIM)
    writes = conv_out[:, INNER:INNER + STATE]
    readout = conv_out[:, INNER + STATE:]
    deltas = jax.nn.softplus(dt_raw + dt_bias)
    decays = -deltas * jnp.exp(a_log)
    return (values, writes, readout, deltas, decays)

def gate_norm(ssd_out, gate_in, gate_gain):
    gated = ssd_out.reshape(gate_in.shape) * jax.nn.silu(gate_in)
    return gated * lax.rsqrt(lax.optimization_barrier(jnp.mean(gated * gated, axis=-1, keepdims=True)) + EPSILON) * gate_gain

def adam_update(params, grads, first_moment, second_moment):
    new_first = BETA_ONE * first_moment + (1.0 - BETA_ONE) * grads
    new_second = BETA_TWO * second_moment + (1.0 - BETA_TWO) * grads * grads
    corr_one = 1.0 - BETA_ONE ** ADAM_STEP
    corr_two = 1.0 - BETA_TWO ** ADAM_STEP
    update = new_first / corr_one / (jnp.sqrt(new_second / corr_two) + ADAM_EPS)
    new_params = params - LEARN_RATE * (update + DECAY_RATE * params)
    return (new_params, new_first, new_second)

def mix_sequence(xbc_f, gate_f, dtr_f, seg_ids, conv_weight, conv_bias, gate_gain, dt_bias, a_log, d_skip):
    extended = jnp.concatenate([jnp.zeros((CONV_WIDTH - 1, CONV_CH), jnp.float32), xbc_f], 0)
    ext_seg = jnp.concatenate([jnp.full((CONV_WIDTH - 1,), -1, jnp.int32), seg_ids], 0)
    values, writes, readout, deltas, decays = mixer_inputs(extended, ext_seg, dtr_f, conv_weight, conv_bias, dt_bias, a_log)
    zero_state = jnp.zeros((HEADS, HEAD_DIM, STATE), jnp.float32)
    ssd_out, final_state = ssd_scan(values, writes, readout, deltas, decays, seg_ids, jnp.array(-1, jnp.int32), zero_state)
    ssd_out = ssd_out + d_skip[None, :, None] * values
    return gate_norm(ssd_out, gate_f, gate_gain)

def reference(tokens, cotangent, segments, params, first_moment, second_moment):
    w_in, w_out, conv_w, conv_b, norm_gain, gate_gain, dt_bias, a_log, d_skip = unpack(params.astype(jnp.bfloat16))
    small_f = [piece.astype(jnp.float32) for piece in (conv_w, conv_b, gate_gain, dt_bias, a_log, d_skip)]
    norm_f = norm_gain.astype(jnp.float32)
    seq_count = tokens.shape[0] // SEQ_LEN

    def per_sequence(grad_sums, inputs):
        seq_tok, seq_cot, seq_ids = inputs
        tok_f = seq_tok.astype(jnp.float32)
        inverse = lax.rsqrt(lax.optimization_barrier(jnp.mean(tok_f * tok_f, axis=-1, keepdims=True)) + EPSILON)
        normed = tok_f * inverse
        hidden_in = (normed * norm_f).astype(jnp.bfloat16)
        projected = jnp.dot(hidden_in, w_in, preferred_element_type=jnp.float32).astype(jnp.bfloat16)
        gate_in = projected[:, :INNER].astype(jnp.float32)
        xbc_f = projected[:, INNER:INNER + CONV_CH].astype(jnp.float32)
        dt_raw = projected[:, INNER + CONV_CH:].astype(jnp.float32)

        def mixer_fn(xbc_in, gate_arg, dtr_arg, conv_weight, conv_bias, gain_arg, bias_arg, alog_arg, skip_arg):
            return mix_sequence(xbc_in, gate_arg, dtr_arg, seq_ids, conv_weight, conv_bias, gain_arg, bias_arg, alog_arg, skip_arg)
        mixed_f, mixer_vjp = jax.vjp(mixer_fn, xbc_f, gate_in, dt_raw, *small_f)
        mixed_out = mixed_f.astype(jnp.bfloat16)
        output = (tok_f + jnp.dot(mixed_out, w_out, preferred_element_type=jnp.float32)).astype(jnp.bfloat16)
        grad_w_out = jnp.dot(mixed_out.T, seq_cot, preferred_element_type=jnp.float32)
        grad_mixed = jnp.dot(seq_cot, w_out.T, preferred_element_type=jnp.float32)
        grads_mix = mixer_vjp(grad_mixed)
        grad_proj = jnp.concatenate([grads_mix[1], grads_mix[0], grads_mix[2]], 1).astype(jnp.bfloat16)
        grad_w_in = jnp.dot(hidden_in.T, grad_proj, preferred_element_type=jnp.float32)
        grad_hidden = jnp.dot(grad_proj, w_in.T, preferred_element_type=jnp.float32)
        grad_gain = lax.optimization_barrier(jnp.sum(grad_hidden * normed, axis=0))
        scaled = grad_hidden * norm_f
        input_grad = seq_cot.astype(jnp.float32) + inverse * (scaled - normed * lax.optimization_barrier(jnp.mean(scaled * normed, axis=-1, keepdims=True)))
        terms = (grad_w_in, grad_w_out, grads_mix[3], grads_mix[4], grad_gain, grads_mix[5], grads_mix[6], grads_mix[7], grads_mix[8])
        new_sums = tuple((running + term_part for running, term_part in zip(grad_sums, terms)))
        return (new_sums, (output, input_grad))
    initial = tuple((jnp.zeros(block_shape, jnp.float32) for block_shape in param_shapes()))
    grad_sums, (outputs, input_grads) = lax.scan(per_sequence, initial, (tokens.reshape(seq_count, SEQ_LEN, D), cotangent.reshape(seq_count, SEQ_LEN, D), segments.reshape(seq_count, SEQ_LEN)))
    grads = jnp.concatenate([running.reshape(-1) for running in grad_sums] + [jnp.zeros((P_TOTAL - P_RAW,), jnp.float32)])
    new_params, new_first, new_second = adam_update(params, grads, first_moment, second_moment)
    return (outputs.reshape(TOKENS, D), input_grads.reshape(TOKENS, D), grads, new_params, new_first, new_second)
```

```python
import functools
import math

import jax
import jax.numpy as jnp
from jax import lax
from jax.experimental import pallas as pl
from jax.experimental.pallas import tpu as pltpu
from jax.sharding import PartitionSpec as P

D = 1024
INNER = 2048
HEADS = 32
HEAD_DIM = 64
STATE = 128
CONV_WIDTH = 4
STRETCH = 256
ADAM_STEP = 3
E_IN = 4384
CONV_CH = 2304
P_RAW = 6601056
P_TOTAL = 6602752


EPSILON = 1e-05
BETA_ONE = 0.9
BETA_TWO = 0.95
LEARN_RATE = 0.003
DECAY_RATE = 0.1
ADAM_EPS = 1e-08
HIGHEST = lax.Precision.HIGHEST


def shifted(shard, axis, by):
    devices = lax.axis_size(axis)
    pairs = [(i, i + by) for i in range(devices) if 0 <= i + by < devices]
    return lax.ppermute(shard, axis, pairs)


SCALE_ROWS = 16


def swap_heads(blocks):
    return lax.all_to_all(blocks, "grp", split_axis=0, concat_axis=0, tiled=True)


STATE_SCALE = 1.0 / 16


def to_state(values):
    return (values * STATE_SCALE).astype(jnp.float16)


def from_state(values):
    return values.astype(jnp.float32) * (1.0 / STATE_SCALE)


def states_before(own_state, through, filler):
    count = lax.axis_size("grp")
    high = through.astype(jnp.bfloat16).astype(jnp.float32)
    low = through - high
    row = lax.broadcasted_iota(jnp.int32, (1, SCALE_ROWS, 1), 1)
    scale = jnp.where(row == 0, high[:, None, None], low[:, None, None])
    scale = jnp.broadcast_to(scale, (HEADS, SCALE_ROWS, STATE))
    arrived = swap_heads(to_state(jnp.concatenate([own_state, scale], 1)))
    arrived, filler = lax.optimization_barrier((arrived, filler))
    arrived = from_state(arrived)
    arrived = arrived.reshape(count, HEADS // count, HEAD_DIM + SCALE_ROWS, STATE)
    throughs = arrived[:, :, HEAD_DIM : HEAD_DIM + 1] + arrived[:, :, HEAD_DIM + 1 : HEAD_DIM + 2]
    state = jnp.zeros((HEADS // count, HEAD_DIM, STATE), jnp.float32)
    before = []
    for place in range(count):
        before.append(to_state(state))
        state = throughs[place] * state + arrived[place, :, :HEAD_DIM]
    return from_state(swap_heads(jnp.concatenate(before))), throughs, filler


def grads_after(own_grad, throughs, filler):
    count = lax.axis_size("grp")
    arrived = swap_heads(to_state(own_grad))
    arrived, filler = lax.optimization_barrier((arrived, filler))
    arrived = from_state(arrived)
    arrived = arrived.reshape(count, HEADS // count, HEAD_DIM, STATE)
    grad = jnp.zeros((HEADS // count, HEAD_DIM, STATE), jnp.float32)
    after = [None] * count
    for place in reversed(range(count)):
        after[place] = to_state(grad)
        grad = throughs[place] * grad + arrived[place]
    return from_state(swap_heads(jnp.concatenate(after))), filler


def param_shapes():
    return [
        (D, E_IN),
        (INNER, D),
        (CONV_WIDTH, CONV_CH),
        (CONV_CH,),
        (D,),
        (INNER,),
        (HEADS,),
        (HEADS,),
        (HEADS,),
    ]


def adam_update(params, grads, first_moment, second_moment):
    new_first = BETA_ONE * first_moment + (1.0 - BETA_ONE) * grads
    new_second = BETA_TWO * second_moment + (1.0 - BETA_TWO) * grads * grads
    corr_one = 1.0 - BETA_ONE**ADAM_STEP
    corr_two = 1.0 - BETA_TWO**ADAM_STEP
    update = new_first / corr_one / (jnp.sqrt(new_second / corr_two) + ADAM_EPS)
    new_params = params - LEARN_RATE * (update + DECAY_RATE * params)
    return (new_params, new_first, new_second)


LANES = 128
ROW_ALIGN = 16


def piece_rows(shard_rows):
    pieces = lax.axis_size("rep")
    return -(-shard_rows // (pieces * ROW_ALIGN)) * ROW_ALIGN


def gather_plan(rows):
    first = rows * GATHER_SHARE // (100 * ROW_ALIGN) * ROW_ALIGN
    second = (rows - first) // (2 * ROW_ALIGN) * ROW_ALIGN
    return first, second, rows - first - second


def gather_params(params):
    shard_rows = params.shape[0] // LANES
    rows = piece_rows(shard_rows)
    pieces = lax.axis_size("rep")
    flat = params.astype(jnp.bfloat16).reshape(shard_rows, LANES)
    flat = jnp.pad(flat, ((0, pieces * rows - shard_rows), (0, 0)))
    own = lax.dynamic_slice_in_dim(flat, lax.axis_index("rep") * rows, rows, 0)
    if shard_rows % ROW_ALIGN:
        return [lax.all_gather(own, ("grp", "rep"), axis=0, tiled=True)]
    cuts = gather_plan(rows)
    most = lax.all_gather(own[: cuts[0]], ("grp", "rep"), axis=0, tiled=True)
    across = collect_stage(own[cuts[0] : cuts[0] + cuts[1]], "grp", 0)
    across = collect_stage(collect_stage(across, "rep", 0), "grp", 1)
    down = collect_stage(own[cuts[0] + cuts[1] :], "grp", 0)
    down = collect_stage(collect_stage(down, "grp", 1), "rep", 0)
    return [
        most,
        collect_stage(across, "rep", 1).reshape(-1, LANES),
        collect_stage(down, "rep", 1).reshape(-1, LANES),
    ]


def locate_rows(first, count):
    groups, pieces = lax.axis_size("grp"), lax.axis_size("rep")
    shard_rows = P_TOTAL // LANES // groups
    rows = piece_rows(shard_rows)
    cuts = gather_plan(rows)
    deep, wide = axis_split("grp")
    across, cores = axis_split("rep")
    found = []
    row = first
    while row < first + count:
        shard, inside = row // shard_rows, row % shard_rows
        piece, within = inside // rows, inside % rows
        part, start = 0, 0
        while within >= start + cuts[part]:
            start += cuts[part]
            part += 1
        size = min(
            start + cuts[part] - within, rows - within, (shard + 1) * shard_rows - row, first + count - row
        )
        z, y, x, c = shard // wide, shard % wide, piece // cores, piece % cores
        block = (
            shard * pieces + piece,
            ((c * wide + y) * across + x) * deep + z,
            ((c * across + x) * wide + y) * deep + z,
        )[part]
        found.append((part, block * cuts[part] + within - start, row - first, size))
        row += size
    return tuple(found)


GATHER_SHARE = 60
SEND_SCALE = 1.0 / 64


def to_link(values):
    return (values * SEND_SCALE).astype(jnp.float16)


def from_link(values):
    return values.astype(jnp.float32) * (1.0 / SEND_SCALE)


def axis_split(axis):
    size = lax.axis_size(axis)
    minor = 2 if axis == "rep" else 2 ** (int(math.log2(size)) // 2)
    return size // minor, minor


def link(axis, part, by):
    major, minor = axis_split(axis)
    pairs = []
    for i in range(major):
        for j in range(minor):
            to = ((i + by) % major, j) if part == 0 else (i, (j + by) % minor)
            pairs.append((i * minor + j, to[0] * minor + to[1]))
    return pairs


def place_on(axis, part):
    major, minor = axis_split(axis)
    index = lax.axis_index(axis)
    return index // minor if part == 0 else index % minor


def reduce_stage(data, dim, axis, part, fine=True):
    count = axis_split(axis)[part]
    place = place_on(axis, part)
    total = lax.dynamic_index_in_dim(data, place, dim, False)
    arrived = []
    for by in range(1, count):
        sent = lax.dynamic_index_in_dim(data, (place + by) % count, dim, False)
        sent = to_link(sent) if fine else sent.astype(jnp.bfloat16)
        arrived.append(lax.ppermute(sent, axis, link(axis, part, by)))
    for block in arrived:
        total = total + (from_link(block) if fine else block.astype(jnp.float32))
    return total


def collect_stage(own, axis, part):
    count = axis_split(axis)[part]
    place = place_on(axis, part)
    whole = jnp.zeros((count,) + own.shape, own.dtype)
    whole = lax.dynamic_update_index_in_dim(whole, own, place, 0)
    for by in range(1, count):
        arrived = lax.ppermute(own, axis, link(axis, part, by))
        whole = lax.dynamic_update_index_in_dim(whole, arrived, (place - by) % count, 0)
    return whole


FOLD = LANES // math.gcd(E_IN, LANES)
FOLD_ROWS = D // FOLD
FOLD_SPAN = FOLD * E_IN // LANES
WIDE = -(-(E_IN + (FOLD - 1) * (E_IN % LANES)) // LANES) * LANES
WIDE_STEP = 5
SUBLANES = 8
VMEM_LIMIT = 66_000_000


def fetch_rows(plan, sources, raw, sems):
    copies = [
        pltpu.make_async_copy(
            sources[part].at[pl.ds(start, size)], raw.at[pl.ds(target, size)], sems.at[index]
        )
        for index, (part, start, target, size) in enumerate(plan)
    ]
    for copy in copies:
        copy.start()
    return copies


def widen_rows(copies, raw, flat):
    for copy in copies:
        copy.wait()
    count = raw.shape[0]
    step = 16 * SUBLANES

    def block(index, carry):
        place = pl.ds(pl.multiple_of(index * step, step), step)
        flat[place, :] = raw[place, :].astype(jnp.float32)
        return carry

    lax.fori_loop(0, count // step, block, 0)


def unfold_in_kernel(plan, most_ref, across_ref, down_ref, out_ref, raw, flat, sems):
    copies = fetch_rows(plan, (most_ref, across_ref, down_ref), raw, sems)
    widen_rows(copies, raw, flat)
    lane = lax.broadcasted_iota(jnp.int32, (1, LANES), 1)
    chunks = -(-E_IN // LANES)
    shift = E_IN % LANES

    def block(index, carry):
        rows = pl.multiple_of(index * ROW_ALIGN, ROW_ALIGN)
        for fold in range(FOLD):
            first = fold * E_IN // LANES
            kept = LANES - fold * shift

            def load(chunk):
                return jnp.concatenate(
                    [
                        flat[
                            pl.ds((rows + part) * FOLD_SPAN + first + chunk, SUBLANES, stride=FOLD_SPAN), :
                        ]
                        for part in range(0, ROW_ALIGN, SUBLANES)
                    ]
                )

            def moved(chunk):
                value = load(chunk)
                return value if fold == 0 else pltpu.roll(value, kept, axis=1)

            current = moved(0)
            for chunk in range(chunks):
                value = current
                width = min(LANES, E_IN - chunk * LANES)
                if chunk + 1 < chunks:
                    current = moved(chunk + 1)
                    if fold:
                        value = jnp.where(lane < kept, value, current)
                out_ref[pl.ds(fold * FOLD_ROWS + rows, ROW_ALIGN), chunk * LANES : chunk * LANES + width] = (
                    value[:, :width].astype(jnp.bfloat16)
                )
        return carry

    lax.fori_loop(0, FOLD_ROWS // ROW_ALIGN, block, 0)


def unfold_out_kernel(plan, most_ref, across_ref, down_ref, out_ref, raw, flat, sems):
    copies = fetch_rows(plan, (most_ref, across_ref, down_ref), raw, sems)
    widen_rows(copies, raw, flat)
    per_row = D // LANES

    def block(index, carry):
        rows = pl.multiple_of(index * ROW_ALIGN, ROW_ALIGN)
        for chunk in range(per_row):
            value = jnp.concatenate(
                [
                    flat[pl.ds((rows + part) * per_row + chunk, SUBLANES, stride=per_row), :]
                    for part in range(0, ROW_ALIGN, SUBLANES)
                ]
            )
            out_ref[pl.ds(rows, ROW_ALIGN), chunk * LANES : (chunk + 1) * LANES] = value.astype(jnp.bfloat16)
        return carry

    lax.fori_loop(0, INNER // ROW_ALIGN, block, 0)


def unfold_call(kernel, name, gathered, first, shape):
    rows = shape[0] * shape[1] // LANES
    plan = locate_rows(first, rows)
    return pl.pallas_call(
        functools.partial(kernel, plan),
        out_shape=jax.ShapeDtypeStruct(shape, jnp.bfloat16),
        in_specs=[pl.BlockSpec(memory_space=pl.ANY)] * len(gathered),
        out_specs=pl.BlockSpec(memory_space=pltpu.VMEM),
        scratch_shapes=[
            pltpu.VMEM((rows, LANES), jnp.bfloat16),
            pltpu.VMEM((rows, LANES), jnp.float32),
            pltpu.SemaphoreType.DMA((len(plan),)),
        ],
        compiler_params=pltpu.CompilerParams(vmem_limit_bytes=VMEM_LIMIT),
        cost_estimate=pl.CostEstimate(flops=rows * LANES, bytes_accessed=8 * rows * LANES, transcendentals=0),
        name=name,
    )(*gathered)


def unpack_weights(gathered):
    shard_rows = P_TOTAL // LANES // lax.axis_size("grp")
    padded_rows = lax.axis_size("rep") * piece_rows(shard_rows)
    in_rows = D * E_IN // LANES
    base = in_rows + INNER * D // LANES
    if shard_rows % ROW_ALIGN == 0:
        w_in = unfold_call(unfold_in_kernel, "unfold_in", gathered, 0, (D, E_IN))
        w_out = unfold_call(unfold_out_kernel, "unfold_out", gathered, in_rows, (INNER, D))
        small = jnp.concatenate(
            [
                gathered[part][start : start + size]
                for part, start, _, size in locate_rows(base, P_TOTAL // LANES - base)
            ]
        )
    else:
        flat = gathered[0].reshape(lax.axis_size("grp"), padded_rows, LANES)
        flat = flat[:, :shard_rows].reshape(-1, LANES)
        w_in = flat[:in_rows].reshape(FOLD_ROWS, FOLD, E_IN)
        w_in = jnp.swapaxes(w_in, 0, 1).reshape(D, E_IN)
        w_out = flat[in_rows:base].reshape(INNER, D)
        small = flat[base:]
    small = small.reshape(-1)
    pieces = []
    offset = 0
    for block_shape in param_shapes()[2:]:
        entries = math.prod(block_shape)
        pieces.append(small[offset : offset + entries].reshape(block_shape))
        offset = offset + entries
    return [w_in, w_out] + pieces


def fold_picks():
    wanted = lax.broadcasted_iota(jnp.int32, (D, D), 1)
    source = lax.broadcasted_iota(jnp.int32, (D, D), 0)
    return (source == FOLD * (wanted % FOLD_ROWS) + wanted // FOLD_ROWS).astype(jnp.bfloat16)


def out_grad_kernel(mixed_ref, cot_ref, out_ref):
    per_row = D // LANES
    block = 256

    def out_block(index, carry):
        columns = pl.multiple_of(index * block, block)
        product = lax.dot_general(
            mixed_ref[:, pl.ds(columns, block)], cot_ref[...],
            (((0,), (0,)), ((), ())), preferred_element_type=jnp.float32,
        )
        for row in range(0, block, SUBLANES):
            for chunk in range(per_row):
                start = (index * block + row) * per_row + chunk
                out_ref[pl.ds(start, SUBLANES, stride=per_row), :] = product[
                    row : row + SUBLANES, chunk * LANES : (chunk + 1) * LANES
                ]
        return carry

    lax.fori_loop(0, INNER // block, out_block, 0)


def out_grad_rows(mixed_out, cotangent):
    inside = pl.BlockSpec(memory_space=pltpu.VMEM)
    rows = INNER * D // LANES
    return pl.pallas_call(
        out_grad_kernel,
        out_shape=jax.ShapeDtypeStruct((rows, LANES), jnp.float32),
        in_specs=[inside] * 2,
        out_specs=inside,
        compiler_params=pltpu.CompilerParams(vmem_limit_bytes=VMEM_LIMIT),
        cost_estimate=pl.CostEstimate(
            flops=2 * INNER * D * cotangent.shape[0], bytes_accessed=INNER * D * 4, transcendentals=0
        ),
        name="out_grad",
    )(mixed_out, cotangent)


def flatten_kernel(
    plan, core_ref, left_ref, proj_ref, small_ref, rows_ref, *refs
):
    groups, across, cores, shard_rows, rows, parts = plan
    targets, (flat, moved, sems) = refs[:-3], refs[-3:]
    out_base = D * E_IN // LANES
    small_base = out_base + INNER * D // LANES
    core = core_ref[0]
    early = pltpu.make_async_copy(
        rows_ref, flat.at[pl.ds(out_base, small_base - out_base)], sems.at[sems.shape[0] - 1]
    )
    early.start()

    steps = WIDE // (LANES * WIDE_STEP)

    def shift_rows(fold, index, carry):
        place = pl.ds(pl.multiple_of(index * ROW_ALIGN, ROW_ALIGN), ROW_ALIGN)
        value = proj_ref[place, :]
        if fold:
            value = pltpu.roll(value.astype(jnp.float32), fold * (E_IN % LANES), axis=1)
        moved[place, :] = value.astype(jnp.bfloat16)
        return carry

    def in_block(fold, step, carry):
        columns = pl.multiple_of(step * (LANES * WIDE_STEP), LANES)
        product = jnp.dot(
            left_ref[fold], moved[:, pl.ds(columns, LANES * WIDE_STEP)],
            preferred_element_type=jnp.float32,
        )
        first = fold * E_IN // LANES + step * WIDE_STEP
        for row in range(0, FOLD_ROWS, SUBLANES):
            for chunk in range(WIDE_STEP):
                place = pl.ds(row * FOLD_SPAN + first + chunk, SUBLANES, stride=FOLD_SPAN)
                value = product[row : row + SUBLANES, chunk * LANES : (chunk + 1) * LANES]
                if fold and chunk == 0:
                    value = value + jnp.where(step == 0, flat[place, :], 0.0)
                flat[place, :] = value
        return carry

    copies = []

    def emit(group):
        for side in range(across):
            given = pl.multiple_of(
                group * shard_rows + (side * cores + 1 - core) * rows, SUBLANES
            )
            kept = pl.multiple_of(group * shard_rows + (side * cores + core) * rows, SUBLANES)
            moves = []
            offset = 0
            for index, part in enumerate(parts):
                for base, target in ((given, targets[index]), (kept, targets[len(parts) + index])):
                    place = pl.ds(pl.multiple_of(base + offset, SUBLANES), part)
                    moves.append((flat.at[place], target.at[group, side]))
                offset += part
            for source, target in moves:
                copy = pltpu.make_async_copy(source, target, sems.at[len(copies)])
                copy.start()
                copies.append(copy)

    flat[pl.ds(small_base, LANES), :] = small_ref[...]
    tail = flat.shape[0] - small_base - LANES
    flat[pl.ds(small_base + LANES, tail), :] = jnp.zeros((tail, LANES), jnp.float32)
    ready = -(-out_base // shard_rows)
    for fold in range(FOLD):
        lax.fori_loop(0, moved.shape[0] // ROW_ALIGN, functools.partial(shift_rows, fold), 0)
        lax.fori_loop(0, steps, functools.partial(in_block, fold), 0)
        if fold == 0:
            early.wait()
            for group in range(ready, groups):
                emit(group)
    for group in range(ready - 1):
        emit(group)
    emit(ready - 1)
    for copy in copies:
        copy.wait()


def row_parts(rows):
    part = rows // (4 * ROW_ALIGN) * ROW_ALIGN
    return (part, part, part, rows - 3 * part)


def flatten_grads(left, proj_grad, small, out_rows):
    groups, pieces = lax.axis_size("grp"), lax.axis_size("rep")
    across, cores = axis_split("rep")
    shard_rows = P_TOTAL // LANES // groups
    rows = piece_rows(shard_rows)
    parts = row_parts(rows)
    plan = (groups, across, cores, shard_rows, rows, parts)
    core = place_on("rep", 1).reshape(1).astype(jnp.int32)
    anywhere = pl.BlockSpec(memory_space=pl.ANY)
    inside = pl.BlockSpec(memory_space=pltpu.VMEM)
    shapes = [
        jax.ShapeDtypeStruct((groups, across, part, LANES), jnp.float32)
        for _ in range(2)
        for part in parts
    ]
    moved = P_TOTAL * 4
    return pl.pallas_call(
        functools.partial(flatten_kernel, plan),
        out_shape=shapes,
        in_specs=[pl.BlockSpec(memory_space=pltpu.SMEM)] + [inside] * 3 + [anywhere],
        out_specs=[anywhere] * len(shapes),
        scratch_shapes=[
            pltpu.VMEM(((groups - 1) * shard_rows + pieces * rows, LANES), jnp.float32),
            pltpu.VMEM((proj_grad.shape[0], WIDE), jnp.bfloat16),
            pltpu.SemaphoreType.DMA((groups * across * len(shapes) + 1,)),
        ],
        compiler_params=pltpu.CompilerParams(vmem_limit_bytes=VMEM_LIMIT),
        cost_estimate=pl.CostEstimate(
            flops=2 * D * E_IN * proj_grad.shape[0], bytes_accessed=moved, transcendentals=0
        ),
        name="flatten",
    )(core, left, proj_grad, small, out_rows)


def core_sum(sent, kept):
    arrived = lax.ppermute(sent, "rep", link("rep", 1, 1))
    return kept + arrived


def core_sums(left, proj_grad, small, out_rows):
    groups, pieces = lax.axis_size("grp"), lax.axis_size("rep")
    across, cores = axis_split("rep")
    shard_rows = P_TOTAL // LANES // groups
    rows = piece_rows(shard_rows)
    parts = row_parts(rows)
    if shard_rows % ROW_ALIGN == 0:
        proj_grad = jnp.pad(proj_grad, ((0, 0), (0, WIDE - E_IN)))
        made = flatten_grads(left, proj_grad, small, out_rows)
        return [core_sum(made[i], made[len(parts) + i]) for i in range(len(parts))]
    grad_w_in = jnp.einsum("fit,tc->ifc", left, proj_grad, preferred_element_type=jnp.float32)
    full_grad = jnp.concatenate([grad_w_in.reshape(-1, LANES), out_rows, small])
    padded = jnp.pad(
        full_grad.reshape(groups, shard_rows, LANES),
        ((0, 0), (0, pieces * rows - shard_rows), (0, 0)),
    ).reshape(groups, across, cores, rows, LANES)
    sums = []
    offset = 0
    for part in parts:
        sums.append(reduce_stage(padded[:, :, :, offset : offset + part], 2, "rep", 1))
        offset += part
    return sums


def sum_grads(*sources):
    deep, wide = axis_split("grp")
    own = []
    for index, part in enumerate(core_sums(*sources)):
        part = part.reshape((deep, wide) + part.shape[1:])
        if index % 2:
            part = reduce_stage(part, 1, "grp", 1)
            part = reduce_stage(part, 1, "rep", 0)
        else:
            part = reduce_stage(part, 2, "rep", 0)
            part = reduce_stage(part, 1, "grp", 1)
        own.append(reduce_stage(part, 0, "grp", 0))
    shard = collect_stage(to_link(jnp.concatenate(own)), "rep", 0)
    shard = collect_stage(shard, "rep", 1)
    shard = jnp.swapaxes(shard, 0, 1).reshape(-1, LANES)
    return from_link(shard[: P_TOTAL // LANES // lax.axis_size("grp")].reshape(-1))


PAIR = LANES // HEAD_DIM
PAIRS = HEADS // PAIR


def bf16_terms(value, count):
    terms = []
    for _ in range(count):
        terms.append(value.astype(jnp.bfloat16))
        value = value - terms[-1].astype(jnp.float32)
    return terms


def terms_dot(left, right, dims, order):
    total = None
    for i, one in reversed(list(enumerate(left))):
        for j, two in reversed(list(enumerate(right))):
            if i + j < order:
                part = lax.dot_general(
                    one, two, (dims, ((), ())), preferred_element_type=jnp.float32
                )
                total = part if total is None else total + part
    return total


def exact_dot(left, right, dims=((1,), (0,))):
    return terms_dot(bf16_terms(left, 2), bf16_terms(right, 2), dims, 2)


def pick_dot(left, picks, dims=((1,), (0,))):
    return terms_dot(bf16_terms(left, 3), [picks], dims, 3)


def head_of_channel(transposed):
    shape = (INNER, LANES) if transposed else (LANES, INNER)
    head = lax.broadcasted_iota(jnp.int32, shape, 1 if transposed else 0)
    channel = lax.broadcasted_iota(jnp.int32, shape, 0 if transposed else 1)
    return (channel // HEAD_DIM == head).astype(jnp.bfloat16)


def spread(per_head):
    return pick_dot(per_head, head_of_channel(False))


def gather_heads(per_channel):
    return pick_dot(per_channel, head_of_channel(True))


def sigmoid(value):
    return 1.0 / (1.0 + jnp.exp(-value))


def ordered(length, backward):
    rows = lax.broadcasted_iota(jnp.int32, (length, length), 0)
    cols = lax.broadcasted_iota(jnp.int32, (length, length), 1)
    return ((cols >= rows) if backward else (cols <= rows)).astype(jnp.float32)


def visible(seg_col, seg_row):
    length = seg_col.shape[0]
    return ordered(length, False) * (seg_col == seg_row).astype(jnp.float32)


def end_scale(cum, seg_col):
    last = cum.shape[0] - 1
    to_end = (seg_col == seg_col[last:, :]).astype(jnp.float32)
    return jnp.exp(cum[last:, :] - cum) * to_end


def linked_rows(seg_col, prev_ref):
    return (seg_col == prev_ref[0]).astype(jnp.float32)


def conv_before(ext_ref, same_ref, weight_ref, bias_ref):
    length = same_ref.shape[0]
    total = jnp.broadcast_to(bias_ref[...], (length, ext_ref.shape[1]))
    for tap in range(CONV_WIDTH):
        first = SUBLANES - (CONV_WIDTH - 1) + tap
        total = total + weight_ref[tap : tap + 1, :] * (
            ext_ref[pl.ds(first, length), :] * same_ref[:, tap : tap + 1]
        )
    return total


def states_kernel(
    ext_ref, same_ref, weight_ref, bias_ref, dt_ref, dt_bias_ref, a_log_ref, seg_ref,
    conv_ref, delta_ref, cum_ref, state_ref, weighted,
):
    before = conv_before(ext_ref, same_ref, weight_ref, bias_ref)
    conv_ref[...] = before * sigmoid(before)
    shifted_dt = dt_ref[...] + dt_bias_ref[...]
    delta = jnp.maximum(shifted_dt, 0.0) + jnp.log1p(jnp.exp(-jnp.abs(shifted_dt)))
    delta_ref[...] = delta
    decay = -delta * jnp.exp(a_log_ref[...])
    until = ordered(delta.shape[0], False).astype(jnp.bfloat16)
    cum = terms_dot([until], bf16_terms(decay, 3), ((1,), (0,)), 3)
    cum_ref[...] = cum
    weighted[...] = spread(end_scale(cum, seg_ref[...]) * delta) * conv_ref[:, :INNER]
    writes = conv_ref[:, INNER : INNER + STATE]

    def pair(index, carry):
        chunk = pl.ds(pl.multiple_of(index * LANES, LANES), LANES)
        state_ref[chunk, :] = exact_dot(weighted[:, chunk], writes, ((0,), (0,)))
        return carry

    lax.fori_loop(0, PAIRS, pair, 0)


def head_half(half):
    lane = lax.broadcasted_iota(jnp.int32, (1, LANES), 1)
    return (lane // HEAD_DIM == half).astype(jnp.float32)


def inner_kernel(conv_ref, delta_ref, cum_ref, seg_ref, seg_row_ref, skip_ref, out_ref, wide_cum, wide_delta, cum_t, scores, allowed):
    wide_cum[...] = spread(cum_ref[...])
    wide_delta[...] = spread(delta_ref[...])
    cum_t[...] = cum_ref[...].T
    writes = conv_ref[:, INNER : INNER + STATE]
    reads = conv_ref[:, INNER + STATE :]
    allowed[...] = visible(seg_ref[...], seg_row_ref[...])
    scores[...] = exact_dot(reads, writes, ((1,), (1,)))

    def pair(index, carry):
        chunk = pl.ds(pl.multiple_of(index * LANES, LANES), LANES)
        values = conv_ref[:, chunk]
        scaled = values * wide_delta[:, chunk]
        columns = wide_cum[:, chunk]
        scaled = bf16_terms(scaled, 2)
        total = skip_ref[:, chunk] * values
        for half in range(PAIR):
            column = columns[:, half * HEAD_DIM : half * HEAD_DIM + 1]
            row = cum_t[pl.ds(index * PAIR + half, 1), :]
            mixing = jnp.exp((column - row) * allowed[...]) * allowed[...] * scores[...]
            own = [term * head_half(half).astype(jnp.bfloat16) for term in scaled]
            total = total + terms_dot(bf16_terms(mixing, 2), own, ((1,), (0,)), 2)
        out_ref[:, chunk] = total
        return carry

    lax.fori_loop(0, PAIRS, pair, 0)


def gate_kernel(
    out_ref, state_ref, conv_ref, cum_ref, seg_ref, prev_ref, gate_ref, grad_mixed_ref, gain_ref,
    mixed_ref, grad_ssd_ref, grad_gate_ref, own_grad_ref, grad_gain_ref, grad_cum_ref, grad_reads_ref,
    factored, ssd,
):
    reads = conv_ref[:, INNER + STATE :]
    factor = spread(linked_rows(seg_ref[...], prev_ref) * jnp.exp(cum_ref[...]))
    carried = exact_dot(reads, state_ref[...], ((1,), (1,))) * factor
    ssd[...] = out_ref[...] + carried
    gate = gate_ref[...].astype(jnp.float32)
    opened = sigmoid(gate)
    silu = gate * opened
    gated = ssd[...] * silu
    scale = lax.rsqrt(jnp.mean(gated * gated, axis=-1, keepdims=True) + EPSILON)
    mixed_ref[...] = (gated * scale * gain_ref[...]).astype(jnp.bfloat16)
    grad_mixed = grad_mixed_ref[...]
    grad_gain_ref[...] = jnp.sum(grad_mixed * gated * scale, axis=0, keepdims=True)
    inner = grad_mixed * gain_ref[...]
    grad_gated = scale * inner - gated * (
        scale * scale * scale * jnp.mean(inner * gated, axis=-1, keepdims=True)
    )
    grad_ssd = grad_gated * silu
    grad_ssd_ref[...] = grad_ssd
    grad_gate_ref[...] = (
        grad_gated * ssd[...] * (opened * (1.0 + gate * (1.0 - opened)))
    ).astype(jnp.bfloat16)
    grad_cum_ref[...] = gather_heads(grad_ssd * carried)
    factored[...] = grad_ssd * factor
    grad_reads_ref[...] = exact_dot(factored[...], state_ref[...])

    def pair(index, carry):
        chunk = pl.ds(pl.multiple_of(index * LANES, LANES), LANES)
        own_grad_ref[chunk, :] = exact_dot(factored[:, chunk], reads, ((0,), (0,)))
        return carry

    lax.fori_loop(0, PAIRS, pair, 0)


def inner_grad_kernel(
    grad_ssd_ref, conv_ref, delta_ref, cum_ref, seg_ref, seg_row_ref, skip_ref, cum_in_ref, reads_in_ref,
    grad_values_ref, grad_cum_ref, grad_delta_ref, grad_writes_ref, grad_reads_ref, grad_skip_ref,
    wide_cum, wide_delta, cum_t, scores, allowed, grad_scores, by_delta, grad_cum_t,
):
    wide_cum[...] = spread(cum_ref[...])
    wide_delta[...] = spread(delta_ref[...])
    cum_t[...] = cum_ref[...].T
    writes = conv_ref[:, INNER : INNER + STATE]
    reads = conv_ref[:, INNER + STATE :]
    allowed[...] = visible(seg_ref[...], seg_row_ref[...])
    scores[...] = exact_dot(reads, writes, ((1,), (1,)))
    grad_scores[...] = jnp.zeros_like(grad_scores)
    grad_cum_t[...] = jnp.zeros_like(grad_cum_t)
    grad_cum_ref[...] = cum_in_ref[...]
    lanes = lax.broadcasted_iota(jnp.int32, (1, LANES), 1)

    def pair(index, carry):
        chunk = pl.ds(pl.multiple_of(index * LANES, LANES), LANES)
        values = conv_ref[:, chunk]
        delta = wide_delta[:, chunk]
        scaled = values * delta
        columns = wide_cum[:, chunk]
        grad_out = grad_ssd_ref[:, chunk]
        grad_scaled = jnp.zeros_like(scaled)
        scaled = bf16_terms(scaled, 2)
        grad_terms = bf16_terms(grad_out, 2)
        for half in range(PAIR):
            head = index * PAIR + half
            column = columns[:, half * HEAD_DIM : half * HEAD_DIM + 1]
            row = cum_t[pl.ds(head, 1), :]
            kernel = jnp.exp((column - row) * allowed[...]) * allowed[...]
            mixing = kernel * scores[...]
            part = [term * head_half(half).astype(jnp.bfloat16) for term in grad_terms]
            grad_scaled = grad_scaled + terms_dot(bf16_terms(mixing, 2), part, ((0,), (0,)), 2)
            grad_mixing = terms_dot(part, scaled, ((1,), (1,)), 2)
            grad_scores[...] += grad_mixing * kernel
            grad_gap = grad_mixing * mixing
            later = jnp.sum(grad_gap, axis=1, keepdims=True)
            grad_cum_ref[...] += jnp.where(lanes == head, later, 0.0)
            grad_cum_t[pl.ds(head, 1), :] = jnp.sum(grad_gap, axis=0, keepdims=True)
        grad_values_ref[:, chunk] = grad_scaled * delta + grad_out * skip_ref[:, chunk]
        by_delta[:, chunk] = grad_scaled * values
        grad_skip_ref[:, chunk] = jnp.sum(grad_out * values, axis=0, keepdims=True)
        return carry

    lax.fori_loop(0, PAIRS, pair, 0)
    grad_cum_ref[...] -= grad_cum_t[...].T
    grad_delta_ref[...] = gather_heads(by_delta[...])
    grad_reads_ref[...] = reads_in_ref[...] + exact_dot(grad_scores[...], writes)
    grad_writes_ref[...] = exact_dot(grad_scores[...], reads, ((0,), (0,)))


def conv_grad_kernel(
    after_ref, state_ref, grad_values_ref, grad_writes_ref, grad_reads_ref, grad_cum_ref, grad_delta_ref,
    conv_ref, ext_ref, same_ref, weight_ref, bias_ref, delta_ref, cum_ref, seg_ref, prev_ref,
    dt_ref, dt_bias_ref, a_log_ref,
    grad_ext_ref, grad_weight_ref, grad_bias_ref, grad_dt_ref, grad_a_log_ref, grad_dt_bias_ref,
    grad_conv, from_state_ref,
):
    length = delta_ref.shape[0]
    last = length - 1
    writes = conv_ref[:, INNER : INNER + STATE]
    values = conv_ref[:, :INNER]
    delta = delta_ref[...]
    cum = cum_ref[...]
    shrink = end_scale(cum, seg_ref[...])
    end_weight = spread(shrink * delta)
    from_state_ref[...] = exact_dot(writes, after_ref[...], ((1,), (1,)))
    grad_conv[:, :INNER] = grad_values_ref[...] + from_state_ref[...] * end_weight
    grad_conv[:, INNER : INNER + STATE] = grad_writes_ref[...] + exact_dot(
        values * end_weight, after_ref[...]
    )
    grad_conv[:, INNER + STATE :] = grad_reads_ref[...]
    grad_end = gather_heads(from_state_ref[...] * values)
    grad_delta = grad_delta_ref[...] + grad_end * shrink
    moved = grad_end * (shrink * delta)
    per_channel = jnp.sum(state_ref[...] * after_ref[...], axis=1, keepdims=True)
    kept = jnp.sum(per_channel * head_of_channel(True).astype(jnp.float32), axis=0, keepdims=True)
    linked = linked_rows(seg_ref[...], prev_ref)
    grad_last = jnp.sum(moved, axis=0, keepdims=True) + (
        jnp.exp(cum[last:, :]) * linked[last:, :] * kept
    )
    row = lax.broadcasted_iota(jnp.int32, (length, 1), 0)
    grad_cum = grad_cum_ref[...] - moved + jnp.where(row == last, grad_last, 0.0)
    since = ordered(length, True).astype(jnp.bfloat16)
    grad_decay = terms_dot([since], bf16_terms(grad_cum, 3), ((1,), (0,)), 3)
    rate = jnp.exp(a_log_ref[...])
    grad_a_log_ref[...] = jnp.sum(-grad_decay * delta * rate, axis=0, keepdims=True)
    grad_dt = (grad_delta - grad_decay * rate) * sigmoid(dt_ref[...] + dt_bias_ref[...])
    grad_dt_ref[...] = grad_dt
    grad_dt_bias_ref[...] = jnp.sum(grad_dt, axis=0, keepdims=True)
    before = conv_before(ext_ref, same_ref, weight_ref, bias_ref)
    opened = sigmoid(before)
    grad_before = grad_conv[...] * (opened * (1.0 + before * (1.0 - opened)))
    grad_bias_ref[...] = jnp.sum(grad_before, axis=0, keepdims=True)
    grad_ext_ref[...] = jnp.zeros_like(grad_ext_ref)
    grad_weight_ref[...] = jnp.zeros_like(grad_weight_ref)
    for tap in range(CONV_WIDTH):
        place = pl.ds(SUBLANES - (CONV_WIDTH - 1) + tap, length)
        reached = grad_before * same_ref[:, tap : tap + 1]
        grad_weight_ref[tap : tap + 1, :] = jnp.sum(
            reached * ext_ref[place, :], axis=0, keepdims=True
        )
        grad_ext_ref[place, :] += reached * weight_ref[tap : tap + 1, :]


def local_call(kernel, shapes, scratch, name, flops, *args):
    spaces = [
        pl.BlockSpec(memory_space=pltpu.SMEM if arg.dtype == jnp.int32 and arg.ndim == 1 else pltpu.VMEM)
        for arg in args
    ]
    return pl.pallas_call(
        kernel,
        out_shape=[jax.ShapeDtypeStruct(*shape) for shape in shapes],
        in_specs=spaces,
        out_specs=[pl.BlockSpec(memory_space=pltpu.VMEM)] * len(shapes),
        scratch_shapes=[pltpu.VMEM(*shape) for shape in scratch],
        compiler_params=pltpu.CompilerParams(vmem_limit_bytes=VMEM_LIMIT),
        cost_estimate=pl.CostEstimate(
            flops=flops, bytes_accessed=sum(a.size * a.dtype.itemsize for a in args), transcendentals=0
        ),
        name=name,
    )(*args)


def f32(*shape):
    return (shape, jnp.float32)


def bf16(*shape):
    return (shape, jnp.bfloat16)


def pad_heads(array):
    return jnp.pad(array, [(0, 0)] * (array.ndim - 1) + [(0, LANES - HEADS)])


def on_device(tokens, cotangent, segments, params, first_moment, second_moment):
    length = tokens.shape[0]
    lag_rows = CONV_WIDTH - 1
    gathered = gather_params(params)
    picks = fold_picks()
    tail_tok, tail_seg = shifted((tokens[length - lag_rows :], segments[length - lag_rows :]), "grp", 1)
    ext_tok = jnp.concatenate(
        [jnp.zeros((ROW_ALIGN - lag_rows, D), tokens.dtype), tail_tok, tokens], 0
    )
    tok_f = jnp.dot(ext_tok, picks, preferred_element_type=jnp.float32)
    inverse = lax.rsqrt(jnp.mean(tok_f * tok_f, axis=-1, keepdims=True) + EPSILON)
    normed = tok_f * inverse
    w_in, w_out, conv_w, conv_b, norm_gain, gate_gain, dt_bias, a_log, d_skip = unpack_weights(gathered)
    conv_w_f = jnp.pad(conv_w.astype(jnp.float32), ((0, SUBLANES - CONV_WIDTH), (0, 0)))
    conv_b_f = conv_b.astype(jnp.float32)[None]
    gate_gain_f = gate_gain.astype(jnp.float32)[None]
    dt_bias_f = pad_heads(dt_bias.astype(jnp.float32)[None])
    a_log_f = pad_heads(a_log.astype(jnp.float32)[None])
    d_skip_f = jnp.repeat(d_skip.astype(jnp.float32), HEAD_DIM)[None]
    norm_f = norm_gain.astype(jnp.float32).reshape(FOLD_ROWS, FOLD).T.reshape(-1)
    hidden_in = (normed * norm_f).astype(jnp.bfloat16)
    projected = jnp.dot(hidden_in, w_in, preferred_element_type=jnp.float32).astype(jnp.bfloat16)
    hidden_in, normed, inverse = hidden_in[ROW_ALIGN:], normed[ROW_ALIGN:], inverse[ROW_ALIGN:]
    gate_in = projected[ROW_ALIGN:, :INNER]
    extended = projected[ROW_ALIGN - SUBLANES :, INNER : INNER + CONV_CH].astype(jnp.float32)
    dt_raw = pad_heads(projected[ROW_ALIGN:, INNER + CONV_CH :].astype(jnp.float32))
    ext_seg = jnp.concatenate([tail_seg, segments], 0)
    prev_seg = tail_seg[lag_rows - 1 :]
    same = jnp.stack(
        [(ext_seg[tap : tap + length] == segments).astype(jnp.float32) for tap in range(CONV_WIDTH)], 1
    )
    seg_col, seg_row = segments[:, None], segments[None]
    square = f32(length, length)
    unit = length * INNER * STATE * 2
    conv_out, delta, cum, own_state = local_call(
        states_kernel,
        [f32(length, CONV_CH), f32(length, LANES), f32(length, LANES), f32(INNER, STATE)],
        [f32(length, INNER)],
        "states", 20 * unit,
        extended, same, conv_w_f, conv_b_f, dt_raw, dt_bias_f, a_log_f, seg_col,
    )
    linked_last = (segments[length - 1] == prev_seg[0]).astype(jnp.float32)
    through = jnp.exp(cum[length - 1, :HEADS]) * linked_last
    grad_mixed = jnp.dot(cotangent, w_out.T, preferred_element_type=jnp.float32)
    state_in, throughs, grad_mixed = states_before(
        own_state.reshape(HEADS, HEAD_DIM, STATE), through, grad_mixed
    )
    state_in = state_in.reshape(INNER, STATE)
    (own_out,) = local_call(
        inner_kernel,
        [f32(length, INNER)],
        [f32(length, INNER), f32(length, INNER), f32(LANES, length), square, square],
        "inner", 30 * unit,
        conv_out, delta, cum, seg_col, seg_row, d_skip_f,
    )
    mixed_out, grad_ssd, grad_gate_in, own_grad, grad_gate_gain, grad_cum, grad_reads = local_call(
        gate_kernel,
        [
            bf16(length, INNER), f32(length, INNER), bf16(length, INNER), f32(INNER, STATE),
            f32(1, INNER), f32(length, LANES), f32(length, LANES),
        ],
        [f32(length, INNER), f32(length, INNER)],
        "gate", 30 * unit,
        own_out, state_in, conv_out, cum, seg_col, prev_seg, gate_in, grad_mixed, gate_gain_f,
    )
    grad_state_out, out_rows = grads_after(
        own_grad.reshape(HEADS, HEAD_DIM, STATE), throughs, out_grad_rows(mixed_out, cotangent)
    )
    grad_state_out = grad_state_out.reshape(INNER, STATE)
    activations = (tokens.astype(jnp.float32) + jnp.dot(mixed_out, w_out, preferred_element_type=jnp.float32)).astype(
        jnp.bfloat16
    )
    grad_values, grad_cum, grad_delta, grad_writes, grad_reads, grad_skip = local_call(
        inner_grad_kernel,
        [
            f32(length, INNER), f32(length, LANES), f32(length, LANES), f32(length, STATE),
            f32(length, STATE), f32(1, INNER),
        ],
        [
            f32(length, INNER), f32(length, INNER), f32(LANES, length), square, square, square,
            f32(length, INNER), f32(LANES, length),
        ],
        "inner_grad", 60 * unit,
        grad_ssd, conv_out, delta, cum, seg_col, seg_row, d_skip_f, grad_cum, grad_reads,
    )
    grad_ext, grad_conv_w, grad_conv_b, grad_dtr, grad_a_log, grad_dt_bias = local_call(
        conv_grad_kernel,
        [
            f32(length + SUBLANES, CONV_CH), f32(SUBLANES, CONV_CH), f32(1, CONV_CH),
            f32(length, LANES), f32(1, LANES), f32(1, LANES),
        ],
        [f32(length, CONV_CH), f32(length, INNER)],
        "conv_grad", 30 * unit,
        grad_state_out, state_in, grad_values, grad_writes, grad_reads, grad_cum, grad_delta,
        conv_out, extended, same, conv_w_f, conv_b_f, delta, cum, seg_col, prev_seg,
        dt_raw, dt_bias_f, a_log_f,
    )
    from_next = shifted(grad_ext[SUBLANES - lag_rows : SUBLANES], "grp", -1)
    grad_xbc = grad_ext[SUBLANES:] + jnp.concatenate(
        [jnp.zeros((length - lag_rows, CONV_CH), jnp.float32), from_next], 0
    )
    grad_proj = jnp.concatenate(
        [grad_gate_in, grad_xbc.astype(jnp.bfloat16), grad_dtr[:, :HEADS].astype(jnp.bfloat16)], 1
    )
    grad_hidden = jnp.dot(grad_proj, w_in.T, preferred_element_type=jnp.float32)
    grad_gain = jnp.sum(grad_hidden * normed, axis=0)
    scaled = grad_hidden * norm_f
    input_grad = cotangent.astype(jnp.float32) + lax.dot_general(
        inverse * (scaled - normed * jnp.mean(scaled * normed, axis=-1, keepdims=True)),
        picks.astype(jnp.float32), (((1,), (1,)), ((), ())), precision=HIGHEST,
    )
    terms = (
        grad_conv_w[:CONV_WIDTH],
        grad_conv_b,
        grad_gain.reshape(FOLD, FOLD_ROWS).T,
        grad_gate_gain,
        grad_dt_bias[:, :HEADS],
        grad_a_log[:, :HEADS],
        jnp.sum(grad_skip.reshape(HEADS, HEAD_DIM), axis=1),
        jnp.zeros((P_TOTAL - P_RAW,), jnp.float32),
    )
    small = jnp.concatenate([term_part.reshape(-1) for term_part in terms]).reshape(-1, LANES)
    grad_shard = sum_grads(
        hidden_in.T.reshape(FOLD, FOLD_ROWS, length), grad_proj, small, out_rows
    )
    new_params, new_first, new_second = adam_update(params, grad_shard, first_moment, second_moment)
    return (activations, input_grad, grad_shard, new_params, new_first, new_second)


def solution(mesh):
    placed = (
        P(("rep", "grp"), None),
        P(("rep", "grp"), None),
        P(("rep", "grp")),
        P("grp"),
        P("grp"),
        P("grp"),
    )
    return jax.shard_map(
        on_device,
        mesh=mesh,
        in_specs=placed,
        out_specs=(
            P(("rep", "grp"), None),
            P(("rep", "grp"), None),
            P("grp"),
            P("grp"),
            P("grp"),
            P("grp"),
        ),
        check_vma=False,
    )
```

```python
import functools
import math

import jax
import jax.numpy as jnp
from jax import lax
from jax.experimental import pallas as pl
from jax.experimental.pallas import tpu as pltpu
from jax.sharding import PartitionSpec as P

D = 1024
INNER = 2048
HEADS = 32
HEAD_DIM = 64
STATE = 128
CONV_WIDTH = 4
STRETCH = 256
ADAM_STEP = 3
E_IN = 4384
CONV_CH = 2304
P_RAW = 6601056
P_TOTAL = 6602752


EPSILON = 1e-05
BETA_ONE = 0.9
BETA_TWO = 0.95
LEARN_RATE = 0.003
DECAY_RATE = 0.1
ADAM_EPS = 1e-08
HIGHEST = lax.Precision.HIGHEST


def shifted(shard, axis, by):
    devices = lax.axis_size(axis)
    pairs = [(i, i + by) for i in range(devices) if 0 <= i + by < devices]
    return lax.ppermute(shard, axis, pairs)


SCALE_ROWS = 16


def swap_heads(blocks):
    return lax.all_to_all(blocks, "grp", split_axis=0, concat_axis=0, tiled=True)


STATE_SCALE = 1.0 / 16


def to_state(values):
    return (values * STATE_SCALE).astype(jnp.float16)


def from_state(values):
    return values.astype(jnp.float32) * (1.0 / STATE_SCALE)


def states_before(own_state, through, filler):
    count = lax.axis_size("grp")
    high = through.astype(jnp.bfloat16).astype(jnp.float32)
    low = through - high
    row = lax.broadcasted_iota(jnp.int32, (1, SCALE_ROWS, 1), 1)
    scale = jnp.where(row == 0, high[:, None, None], low[:, None, None])
    scale = jnp.broadcast_to(scale, (HEADS, SCALE_ROWS, STATE))
    arrived = swap_heads(to_state(jnp.concatenate([own_state, scale], 1)))
    arrived, filler = lax.optimization_barrier((arrived, filler))
    arrived = from_state(arrived)
    arrived = arrived.reshape(count, HEADS // count, HEAD_DIM + SCALE_ROWS, STATE)
    throughs = arrived[:, :, HEAD_DIM : HEAD_DIM + 1] + arrived[:, :, HEAD_DIM + 1 : HEAD_DIM + 2]
    state = jnp.zeros((HEADS // count, HEAD_DIM, STATE), jnp.float32)
    before = []
    for place in range(count):
        before.append(to_state(state))
        state = throughs[place] * state + arrived[place, :, :HEAD_DIM]
    return from_state(swap_heads(jnp.concatenate(before))), throughs, filler


def grads_after(own_grad, throughs, filler):
    count = lax.axis_size("grp")
    arrived = swap_heads(to_state(own_grad))
    arrived, filler = lax.optimization_barrier((arrived, filler))
    arrived = from_state(arrived)
    arrived = arrived.reshape(count, HEADS // count, HEAD_DIM, STATE)
    grad = jnp.zeros((HEADS // count, HEAD_DIM, STATE), jnp.float32)
    after = [None] * count
    for place in reversed(range(count)):
        after[place] = to_state(grad)
        grad = throughs[place] * grad + arrived[place]
    return from_state(swap_heads(jnp.concatenate(after))), filler


def param_shapes():
    return [
        (D, E_IN),
        (INNER, D),
        (CONV_WIDTH, CONV_CH),
        (CONV_CH,),
        (D,),
        (INNER,),
        (HEADS,),
        (HEADS,),
        (HEADS,),
    ]


def adam_update(params, grads, first_moment, second_moment):
    new_first = BETA_ONE * first_moment + (1.0 - BETA_ONE) * grads
    new_second = BETA_TWO * second_moment + (1.0 - BETA_TWO) * grads * grads
    corr_one = 1.0 - BETA_ONE**ADAM_STEP
    corr_two = 1.0 - BETA_TWO**ADAM_STEP
    update = new_first / corr_one / (jnp.sqrt(new_second / corr_two) + ADAM_EPS)
    new_params = params - LEARN_RATE * (update + DECAY_RATE * params)
    return (new_params, new_first, new_second)


LANES = 128
ROW_ALIGN = 16


def piece_rows(shard_rows):
    pieces = lax.axis_size("rep")
    return -(-shard_rows // (pieces * ROW_ALIGN)) * ROW_ALIGN


def gather_plan(rows):
    first = rows * GATHER_SHARE // (100 * ROW_ALIGN) * ROW_ALIGN
    second = (rows - first) // (2 * ROW_ALIGN) * ROW_ALIGN
    return first, second, rows - first - second


def gather_params(params):
    shard_rows = params.shape[0] // LANES
    rows = piece_rows(shard_rows)
    pieces = lax.axis_size("rep")
    flat = params.astype(jnp.bfloat16).reshape(shard_rows, LANES)
    flat = jnp.pad(flat, ((0, pieces * rows - shard_rows), (0, 0)))
    own = lax.dynamic_slice_in_dim(flat, lax.axis_index("rep") * rows, rows, 0)
    if shard_rows % ROW_ALIGN:
        return [lax.all_gather(own, ("grp", "rep"), axis=0, tiled=True)]
    cuts = gather_plan(rows)
    most = lax.all_gather(own[: cuts[0]], ("grp", "rep"), axis=0, tiled=True)
    across = collect_stage(own[cuts[0] : cuts[0] + cuts[1]], "grp", 0)
    across = collect_stage(collect_stage(across, "rep", 0), "grp", 1)
    down = collect_stage(own[cuts[0] + cuts[1] :], "grp", 0)
    down = collect_stage(collect_stage(down, "grp", 1), "rep", 0)
    return [
        most,
        collect_stage(across, "rep", 1).reshape(-1, LANES),
        collect_stage(down, "rep", 1).reshape(-1, LANES),
    ]


def locate_rows(first, count):
    groups, pieces = lax.axis_size("grp"), lax.axis_size("rep")
    shard_rows = P_TOTAL // LANES // groups
    rows = piece_rows(shard_rows)
    cuts = gather_plan(rows)
    deep, wide = axis_split("grp")
    across, cores = axis_split("rep")
    found = []
    row = first
    while row < first + count:
        shard, inside = row // shard_rows, row % shard_rows
        piece, within = inside // rows, inside % rows
        part, start = 0, 0
        while within >= start + cuts[part]:
            start += cuts[part]
            part += 1
        size = min(
            start + cuts[part] - within, rows - within, (shard + 1) * shard_rows - row, first + count - row
        )
        z, y, x, c = shard // wide, shard % wide, piece // cores, piece % cores
        block = (
            shard * pieces + piece,
            ((c * wide + y) * across + x) * deep + z,
            ((c * across + x) * wide + y) * deep + z,
        )[part]
        found.append((part, block * cuts[part] + within - start, row - first, size))
        row += size
    return tuple(found)


GATHER_SHARE = 60
SEND_SCALE = 1.0 / 64


def to_link(values):
    return (values * SEND_SCALE).astype(jnp.float16)


def from_link(values):
    return values.astype(jnp.float32) * (1.0 / SEND_SCALE)


def axis_split(axis):
    size = lax.axis_size(axis)
    minor = 2 if axis == "rep" else 2 ** (int(math.log2(size)) // 2)
    return size // minor, minor


def link(axis, part, by):
    major, minor = axis_split(axis)
    pairs = []
    for i in range(major):
        for j in range(minor):
            to = ((i + by) % major, j) if part == 0 else (i, (j + by) % minor)
            pairs.append((i * minor + j, to[0] * minor + to[1]))
    return pairs


def place_on(axis, part):
    major, minor = axis_split(axis)
    index = lax.axis_index(axis)
    return index // minor if part == 0 else index % minor


def reduce_stage(data, dim, axis, part, fine=True):
    count = axis_split(axis)[part]
    place = place_on(axis, part)
    total = lax.dynamic_index_in_dim(data, place, dim, False)
    arrived = []
    for by in range(1, count):
        sent = lax.dynamic_index_in_dim(data, (place + by) % count, dim, False)
        sent = to_link(sent) if fine else sent.astype(jnp.bfloat16)
        arrived.append(lax.ppermute(sent, axis, link(axis, part, by)))
    for block in arrived:
        total = total + (from_link(block) if fine else block.astype(jnp.float32))
    return total


def collect_stage(own, axis, part):
    count = axis_split(axis)[part]
    place = place_on(axis, part)
    whole = jnp.zeros((count,) + own.shape, own.dtype)
    whole = lax.dynamic_update_index_in_dim(whole, own, place, 0)
    for by in range(1, count):
        arrived = lax.ppermute(own, axis, link(axis, part, by))
        whole = lax.dynamic_update_index_in_dim(whole, arrived, (place - by) % count, 0)
    return whole


FOLD = LANES // math.gcd(E_IN, LANES)
FOLD_ROWS = D // FOLD
FOLD_SPAN = FOLD * E_IN // LANES
WIDE = -(-(E_IN + (FOLD - 1) * (E_IN % LANES)) // LANES) * LANES
WIDE_STEP = 5
SUBLANES = 8
VMEM_LIMIT = 66_000_000


def fetch_rows(plan, sources, raw, sems):
    copies = [
        pltpu.make_async_copy(
            sources[part].at[pl.ds(start, size)], raw.at[pl.ds(target, size)], sems.at[index]
        )
        for index, (part, start, target, size) in enumerate(plan)
    ]
    for copy in copies:
        copy.start()
    return copies


def widen_rows(copies, raw, flat):
    for copy in copies:
        copy.wait()
    count = raw.shape[0]
    step = 16 * SUBLANES

    def block(index, carry):
        place = pl.ds(pl.multiple_of(index * step, step), step)
        flat[place, :] = raw[place, :].astype(jnp.float32)
        return carry

    lax.fori_loop(0, count // step, block, 0)


def unfold_in_kernel(plan, most_ref, across_ref, down_ref, out_ref, raw, flat, sems):
    copies = fetch_rows(plan, (most_ref, across_ref, down_ref), raw, sems)
    widen_rows(copies, raw, flat)
    lane = lax.broadcasted_iota(jnp.int32, (1, LANES), 1)
    chunks = -(-E_IN // LANES)
    shift = E_IN % LANES

    def block(index, carry):
        rows = pl.multiple_of(index * ROW_ALIGN, ROW_ALIGN)
        for fold in range(FOLD):
            first = fold * E_IN // LANES
            kept = LANES - fold * shift

            def load(chunk):
                return jnp.concatenate(
                    [
                        flat[
                            pl.ds((rows + part) * FOLD_SPAN + first + chunk, SUBLANES, stride=FOLD_SPAN), :
                        ]
                        for part in range(0, ROW_ALIGN, SUBLANES)
                    ]
                )

            def moved(chunk):
                value = load(chunk)
                return value if fold == 0 else pltpu.roll(value, kept, axis=1)

            current = moved(0)
            for chunk in range(chunks):
                value = current
                width = min(LANES, E_IN - chunk * LANES)
                if chunk + 1 < chunks:
                    current = moved(chunk + 1)
                    if fold:
                        value = jnp.where(lane < kept, value, current)
                out_ref[pl.ds(fold * FOLD_ROWS + rows, ROW_ALIGN), chunk * LANES : chunk * LANES + width] = (
                    value[:, :width].astype(jnp.bfloat16)
                )
        return carry

    lax.fori_loop(0, FOLD_ROWS // ROW_ALIGN, block, 0)


def unfold_out_kernel(plan, most_ref, across_ref, down_ref, out_ref, raw, flat, sems):
    copies = fetch_rows(plan, (most_ref, across_ref, down_ref), raw, sems)
    widen_rows(copies, raw, flat)
    per_row = D // LANES

    def block(index, carry):
        rows = pl.multiple_of(index * ROW_ALIGN, ROW_ALIGN)
        for chunk in range(per_row):
            value = jnp.concatenate(
                [
                    flat[pl.ds((rows + part) * per_row + chunk, SUBLANES, stride=per_row), :]
                    for part in range(0, ROW_ALIGN, SUBLANES)
                ]
            )
            out_ref[pl.ds(rows, ROW_ALIGN), chunk * LANES : (chunk + 1) * LANES] = value.astype(jnp.bfloat16)
        return carry

    lax.fori_loop(0, INNER // ROW_ALIGN, block, 0)


def unfold_call(kernel, name, gathered, first, shape):
    rows = shape[0] * shape[1] // LANES
    plan = locate_rows(first, rows)
    return pl.pallas_call(
        functools.partial(kernel, plan),
        out_shape=jax.ShapeDtypeStruct(shape, jnp.bfloat16),
        in_specs=[pl.BlockSpec(memory_space=pl.ANY)] * len(gathered),
        out_specs=pl.BlockSpec(memory_space=pltpu.VMEM),
        scratch_shapes=[
            pltpu.VMEM((rows, LANES), jnp.bfloat16),
            pltpu.VMEM((rows, LANES), jnp.float32),
            pltpu.SemaphoreType.DMA((len(plan),)),
        ],
        compiler_params=pltpu.CompilerParams(vmem_limit_bytes=VMEM_LIMIT),
        cost_estimate=pl.CostEstimate(flops=rows * LANES, bytes_accessed=8 * rows * LANES, transcendentals=0),
        name=name,
    )(*gathered)


def unpack_weights(gathered):
    shard_rows = P_TOTAL // LANES // lax.axis_size("grp")
    padded_rows = lax.axis_size("rep") * piece_rows(shard_rows)
    in_rows = D * E_IN // LANES
    base = in_rows + INNER * D // LANES
    if shard_rows % ROW_ALIGN == 0:
        w_in = unfold_call(unfold_in_kernel, "unfold_in", gathered, 0, (D, E_IN))
        w_out = unfold_call(unfold_out_kernel, "unfold_out", gathered, in_rows, (INNER, D))
        small = jnp.concatenate(
            [
                gathered[part][start : start + size]
                for part, start, _, size in locate_rows(base, P_TOTAL // LANES - base)
            ]
        )
    else:
        flat = gathered[0].reshape(lax.axis_size("grp"), padded_rows, LANES)
        flat = flat[:, :shard_rows].reshape(-1, LANES)
        w_in = flat[:in_rows].reshape(FOLD_ROWS, FOLD, E_IN)
        w_in = jnp.swapaxes(w_in, 0, 1).reshape(D, E_IN)
        w_out = flat[in_rows:base].reshape(INNER, D)
        small = flat[base:]
    small = small.reshape(-1)
    pieces = []
    offset = 0
    for block_shape in param_shapes()[2:]:
        entries = math.prod(block_shape)
        pieces.append(small[offset : offset + entries].reshape(block_shape))
        offset = offset + entries
    return [w_in, w_out] + pieces


def fold_picks():
    wanted = lax.broadcasted_iota(jnp.int32, (D, D), 1)
    source = lax.broadcasted_iota(jnp.int32, (D, D), 0)
    return (source == FOLD * (wanted % FOLD_ROWS) + wanted // FOLD_ROWS).astype(jnp.bfloat16)


def out_grad_kernel(mixed_ref, cot_ref, out_ref):
    per_row = D // LANES
    block = 256

    def out_block(index, carry):
        columns = pl.multiple_of(index * block, block)
        product = lax.dot_general(
            mixed_ref[:, pl.ds(columns, block)], cot_ref[...],
            (((0,), (0,)), ((), ())), preferred_element_type=jnp.float32,
        )
        for row in range(0, block, SUBLANES):
            for chunk in range(per_row):
                start = (index * block + row) * per_row + chunk
                out_ref[pl.ds(start, SUBLANES, stride=per_row), :] = product[
                    row : row + SUBLANES, chunk * LANES : (chunk + 1) * LANES
                ]
        return carry

    lax.fori_loop(0, INNER // block, out_block, 0)


def out_grad_rows(mixed_out, cotangent):
    inside = pl.BlockSpec(memory_space=pltpu.VMEM)
    rows = INNER * D // LANES
    return pl.pallas_call(
        out_grad_kernel,
        out_shape=jax.ShapeDtypeStruct((rows, LANES), jnp.float32),
        in_specs=[inside] * 2,
        out_specs=inside,
        compiler_params=pltpu.CompilerParams(vmem_limit_bytes=VMEM_LIMIT),
        cost_estimate=pl.CostEstimate(
            flops=2 * INNER * D * cotangent.shape[0], bytes_accessed=INNER * D * 4, transcendentals=0
        ),
        name="out_grad",
    )(mixed_out, cotangent)


def flatten_kernel(
    plan, core_ref, left_ref, proj_ref, small_ref, rows_ref, *refs
):
    groups, across, cores, shard_rows, rows, parts = plan
    targets, (flat, moved, sems) = refs[:-3], refs[-3:]
    out_base = D * E_IN // LANES
    small_base = out_base + INNER * D // LANES
    core = core_ref[0]
    early = pltpu.make_async_copy(
        rows_ref, flat.at[pl.ds(out_base, small_base - out_base)], sems.at[sems.shape[0] - 1]
    )
    early.start()

    steps = WIDE // (LANES * WIDE_STEP)

    def shift_rows(fold, index, carry):
        place = pl.ds(pl.multiple_of(index * ROW_ALIGN, ROW_ALIGN), ROW_ALIGN)
        value = proj_ref[place, :]
        if fold:
            value = pltpu.roll(value.astype(jnp.float32), fold * (E_IN % LANES), axis=1)
        moved[place, :] = value.astype(jnp.bfloat16)
        return carry

    def in_block(fold, step, carry):
        columns = pl.multiple_of(step * (LANES * WIDE_STEP), LANES)
        product = jnp.dot(
            left_ref[fold], moved[:, pl.ds(columns, LANES * WIDE_STEP)],
            preferred_element_type=jnp.float32,
        )
        first = fold * E_IN // LANES + step * WIDE_STEP
        for row in range(0, FOLD_ROWS, SUBLANES):
            for chunk in range(WIDE_STEP):
                place = pl.ds(row * FOLD_SPAN + first + chunk, SUBLANES, stride=FOLD_SPAN)
                value = product[row : row + SUBLANES, chunk * LANES : (chunk + 1) * LANES]
                if fold and chunk == 0:
                    value = value + jnp.where(step == 0, flat[place, :], 0.0)
                flat[place, :] = value
        return carry

    copies = []

    def emit(group):
        for side in range(across):
            given = pl.multiple_of(
                group * shard_rows + (side * cores + 1 - core) * rows, SUBLANES
            )
            kept = pl.multiple_of(group * shard_rows + (side * cores + core) * rows, SUBLANES)
            moves = []
            offset = 0
            for index, part in enumerate(parts):
                for base, target in ((given, targets[index]), (kept, targets[len(parts) + index])):
                    place = pl.ds(pl.multiple_of(base + offset, SUBLANES), part)
                    moves.append((flat.at[place], target.at[group, side]))
                offset += part
            for source, target in moves:
                copy = pltpu.make_async_copy(source, target, sems.at[len(copies)])
                copy.start()
                copies.append(copy)

    flat[pl.ds(small_base, LANES), :] = small_ref[...]
    tail = flat.shape[0] - small_base - LANES
    flat[pl.ds(small_base + LANES, tail), :] = jnp.zeros((tail, LANES), jnp.float32)
    ready = -(-out_base // shard_rows)
    for fold in range(FOLD):
        lax.fori_loop(0, moved.shape[0] // ROW_ALIGN, functools.partial(shift_rows, fold), 0)
        lax.fori_loop(0, steps, functools.partial(in_block, fold), 0)
        if fold == 0:
            early.wait()
            for group in range(ready, groups):
                emit(group)
    for group in range(ready - 1):
        emit(group)
    emit(ready - 1)
    for copy in copies:
        copy.wait()


def row_parts(rows):
    part = rows // (4 * ROW_ALIGN) * ROW_ALIGN
    return (part, part, part, rows - 3 * part)


def flatten_grads(left, proj_grad, small, out_rows):
    groups, pieces = lax.axis_size("grp"), lax.axis_size("rep")
    across, cores = axis_split("rep")
    shard_rows = P_TOTAL // LANES // groups
    rows = piece_rows(shard_rows)
    parts = row_parts(rows)
    plan = (groups, across, cores, shard_rows, rows, parts)
    core = place_on("rep", 1).reshape(1).astype(jnp.int32)
    anywhere = pl.BlockSpec(memory_space=pl.ANY)
    inside = pl.BlockSpec(memory_space=pltpu.VMEM)
    shapes = [
        jax.ShapeDtypeStruct((groups, across, part, LANES), jnp.float32)
        for _ in range(2)
        for part in parts
    ]
    moved = P_TOTAL * 4
    return pl.pallas_call(
        functools.partial(flatten_kernel, plan),
        out_shape=shapes,
        in_specs=[pl.BlockSpec(memory_space=pltpu.SMEM)] + [inside] * 3 + [anywhere],
        out_specs=[anywhere] * len(shapes),
        scratch_shapes=[
            pltpu.VMEM(((groups - 1) * shard_rows + pieces * rows, LANES), jnp.float32),
            pltpu.VMEM((proj_grad.shape[0], WIDE), jnp.bfloat16),
            pltpu.SemaphoreType.DMA((groups * across * len(shapes) + 1,)),
        ],
        compiler_params=pltpu.CompilerParams(vmem_limit_bytes=VMEM_LIMIT),
        cost_estimate=pl.CostEstimate(
            flops=2 * D * E_IN * proj_grad.shape[0], bytes_accessed=moved, transcendentals=0
        ),
        name="flatten",
    )(core, left, proj_grad, small, out_rows)


def core_sum(sent, kept):
    arrived = lax.ppermute(sent, "rep", link("rep", 1, 1))
    return kept + arrived


def core_sums(left, proj_grad, small, out_rows):
    groups, pieces = lax.axis_size("grp"), lax.axis_size("rep")
    across, cores = axis_split("rep")
    shard_rows = P_TOTAL // LANES // groups
    rows = piece_rows(shard_rows)
    parts = row_parts(rows)
    if shard_rows % ROW_ALIGN == 0:
        proj_grad = jnp.pad(proj_grad, ((0, 0), (0, WIDE - E_IN)))
        made = flatten_grads(left, proj_grad, small, out_rows)
        return [core_sum(made[i], made[len(parts) + i]) for i in range(len(parts))]
    grad_w_in = jnp.einsum("fit,tc->ifc", left, proj_grad, preferred_element_type=jnp.float32)
    full_grad = jnp.concatenate([grad_w_in.reshape(-1, LANES), out_rows, small])
    padded = jnp.pad(
        full_grad.reshape(groups, shard_rows, LANES),
        ((0, 0), (0, pieces * rows - shard_rows), (0, 0)),
    ).reshape(groups, across, cores, rows, LANES)
    sums = []
    offset = 0
    for part in parts:
        sums.append(reduce_stage(padded[:, :, :, offset : offset + part], 2, "rep", 1))
        offset += part
    return sums


def sum_grads(*sources):
    deep, wide = axis_split("grp")
    own = []
    for index, part in enumerate(core_sums(*sources)):
        part = part.reshape((deep, wide) + part.shape[1:])
        if index % 2:
            part = reduce_stage(part, 1, "grp", 1)
            part = reduce_stage(part, 1, "rep", 0)
        else:
            part = reduce_stage(part, 2, "rep", 0)
            part = reduce_stage(part, 1, "grp", 1)
        own.append(reduce_stage(part, 0, "grp", 0))
    shard = collect_stage(to_link(jnp.concatenate(own)), "rep", 0)
    shard = collect_stage(shard, "rep", 1)
    shard = jnp.swapaxes(shard, 0, 1).reshape(-1, LANES)
    return from_link(shard[: P_TOTAL // LANES // lax.axis_size("grp")].reshape(-1))


PAIR = LANES // HEAD_DIM
PAIRS = HEADS // PAIR


def bf16_terms(value, count):
    terms = []
    for _ in range(count):
        terms.append(value.astype(jnp.bfloat16))
        value = value - terms[-1].astype(jnp.float32)
    return terms


def terms_dot(left, right, dims, order):
    total = None
    for i, one in reversed(list(enumerate(left))):
        for j, two in reversed(list(enumerate(right))):
            if i + j < order:
                part = lax.dot_general(
                    one, two, (dims, ((), ())), preferred_element_type=jnp.float32
                )
                total = part if total is None else total + part
    return total


def exact_dot(left, right, dims=((1,), (0,))):
    return terms_dot(bf16_terms(left, 2), bf16_terms(right, 2), dims, 2)


def pick_dot(left, picks, dims=((1,), (0,))):
    return terms_dot(bf16_terms(left, 3), [picks], dims, 3)


def head_of_channel(transposed):
    shape = (INNER, LANES) if transposed else (LANES, INNER)
    head = lax.broadcasted_iota(jnp.int32, shape, 1 if transposed else 0)
    channel = lax.broadcasted_iota(jnp.int32, shape, 0 if transposed else 1)
    return (channel // HEAD_DIM == head).astype(jnp.bfloat16)


def spread(per_head):
    return pick_dot(per_head, head_of_channel(False))


def gather_heads(per_channel):
    return pick_dot(per_channel, head_of_channel(True))


def sigmoid(value):
    return 1.0 / (1.0 + jnp.exp(-value))


def ordered(length, backward):
    rows = lax.broadcasted_iota(jnp.int32, (length, length), 0)
    cols = lax.broadcasted_iota(jnp.int32, (length, length), 1)
    return ((cols >= rows) if backward else (cols <= rows)).astype(jnp.float32)


def visible(seg_col, seg_row):
    length = seg_col.shape[0]
    return ordered(length, False) * (seg_col == seg_row).astype(jnp.float32)


def end_scale(cum, seg_col):
    last = cum.shape[0] - 1
    to_end = (seg_col == seg_col[last:, :]).astype(jnp.float32)
    return jnp.exp(cum[last:, :] - cum) * to_end


def linked_rows(seg_col, prev_ref):
    return (seg_col == prev_ref[0]).astype(jnp.float32)


def conv_before(ext_ref, same_ref, weight_ref, bias_ref):
    length = same_ref.shape[0]
    total = jnp.broadcast_to(bias_ref[...], (length, ext_ref.shape[1]))
    for tap in range(CONV_WIDTH):
        first = SUBLANES - (CONV_WIDTH - 1) + tap
        total = total + weight_ref[tap : tap + 1, :] * (
            ext_ref[pl.ds(first, length), :] * same_ref[:, tap : tap + 1]
        )
    return total


def states_kernel(
    ext_ref, same_ref, weight_ref, bias_ref, dt_ref, dt_bias_ref, a_log_ref, seg_ref,
    conv_ref, delta_ref, cum_ref, state_ref, weighted,
):
    before = conv_before(ext_ref, same_ref, weight_ref, bias_ref)
    conv_ref[...] = before * sigmoid(before)
    shifted_dt = dt_ref[...] + dt_bias_ref[...]
    delta = jnp.maximum(shifted_dt, 0.0) + jnp.log1p(jnp.exp(-jnp.abs(shifted_dt)))
    delta_ref[...] = delta
    decay = -delta * jnp.exp(a_log_ref[...])
    until = ordered(delta.shape[0], False).astype(jnp.bfloat16)
    cum = terms_dot([until], bf16_terms(decay, 3), ((1,), (0,)), 3)
    cum_ref[...] = cum
    weighted[...] = spread(end_scale(cum, seg_ref[...]) * delta) * conv_ref[:, :INNER]
    writes = conv_ref[:, INNER : INNER + STATE]

    def pair(index, carry):
        chunk = pl.ds(pl.multiple_of(index * LANES, LANES), LANES)
        state_ref[chunk, :] = exact_dot(weighted[:, chunk], writes, ((0,), (0,)))
        return carry

    lax.fori_loop(0, PAIRS, pair, 0)


def head_half(half):
    lane = lax.broadcasted_iota(jnp.int32, (1, LANES), 1)
    return (lane // HEAD_DIM == half).astype(jnp.float32)


def inner_kernel(conv_ref, delta_ref, cum_ref, seg_ref, seg_row_ref, skip_ref, out_ref, wide_cum, wide_delta, cum_t, scores, allowed):
    wide_cum[...] = spread(cum_ref[...])
    wide_delta[...] = spread(delta_ref[...])
    cum_t[...] = cum_ref[...].T
    writes = conv_ref[:, INNER : INNER + STATE]
    reads = conv_ref[:, INNER + STATE :]
    allowed[...] = visible(seg_ref[...], seg_row_ref[...])
    scores[...] = exact_dot(reads, writes, ((1,), (1,)))

    def pair(index, carry):
        chunk = pl.ds(pl.multiple_of(index * LANES, LANES), LANES)
        values = conv_ref[:, chunk]
        scaled = values * wide_delta[:, chunk]
        columns = wide_cum[:, chunk]
        scaled = bf16_terms(scaled, 2)
        total = skip_ref[:, chunk] * values
        for half in range(PAIR):
            column = columns[:, half * HEAD_DIM : half * HEAD_DIM + 1]
            row = cum_t[pl.ds(index * PAIR + half, 1), :]
            mixing = jnp.exp((column - row) * allowed[...]) * allowed[...] * scores[...]
            own = [term * head_half(half).astype(jnp.bfloat16) for term in scaled]
            total = total + terms_dot(bf16_terms(mixing, 2), own, ((1,), (0,)), 2)
        out_ref[:, chunk] = total
        return carry

    lax.fori_loop(0, PAIRS, pair, 0)


def gate_kernel(
    out_ref, state_ref, conv_ref, cum_ref, seg_ref, prev_ref, gate_ref, grad_mixed_ref, gain_ref,
    mixed_ref, grad_ssd_ref, grad_gate_ref, own_grad_ref, grad_gain_ref, grad_cum_ref, grad_reads_ref,
    factored, ssd,
):
    reads = conv_ref[:, INNER + STATE :]
    factor = spread(linked_rows(seg_ref[...], prev_ref) * jnp.exp(cum_ref[...]))
    carried = exact_dot(reads, state_ref[...], ((1,), (1,))) * factor
    ssd[...] = out_ref[...] + carried
    gate = gate_ref[...].astype(jnp.float32)
    opened = sigmoid(gate)
    silu = gate * opened
    gated = ssd[...] * silu
    scale = lax.rsqrt(jnp.mean(gated * gated, axis=-1, keepdims=True) + EPSILON)
    mixed_ref[...] = (gated * scale * gain_ref[...]).astype(jnp.bfloat16)
    grad_mixed = grad_mixed_ref[...]
    grad_gain_ref[...] = jnp.sum(grad_mixed * gated * scale, axis=0, keepdims=True)
    inner = grad_mixed * gain_ref[...]
    grad_gated = scale * inner - gated * (
        scale * scale * scale * jnp.mean(inner * gated, axis=-1, keepdims=True)
    )
    grad_ssd = grad_gated * silu
    grad_ssd_ref[...] = grad_ssd
    grad_gate_ref[...] = (
        grad_gated * ssd[...] * (opened * (1.0 + gate * (1.0 - opened)))
    ).astype(jnp.bfloat16)
    grad_cum_ref[...] = gather_heads(grad_ssd * carried)
    factored[...] = grad_ssd * factor
    grad_reads_ref[...] = exact_dot(factored[...], state_ref[...])

    def pair(index, carry):
        chunk = pl.ds(pl.multiple_of(index * LANES, LANES), LANES)
        own_grad_ref[chunk, :] = exact_dot(factored[:, chunk], reads, ((0,), (0,)))
        return carry

    lax.fori_loop(0, PAIRS, pair, 0)


def inner_grad_kernel(
    grad_ssd_ref, conv_ref, delta_ref, cum_ref, seg_ref, seg_row_ref, skip_ref, cum_in_ref, reads_in_ref,
    grad_values_ref, grad_cum_ref, grad_delta_ref, grad_writes_ref, grad_reads_ref, grad_skip_ref,
    wide_cum, wide_delta, cum_t, scores, allowed, grad_scores, by_delta, grad_cum_t,
):
    wide_cum[...] = spread(cum_ref[...])
    wide_delta[...] = spread(delta_ref[...])
    cum_t[...] = cum_ref[...].T
    writes = conv_ref[:, INNER : INNER + STATE]
    reads = conv_ref[:, INNER + STATE :]
    allowed[...] = visible(seg_ref[...], seg_row_ref[...])
    scores[...] = exact_dot(reads, writes, ((1,), (1,)))
    grad_scores[...] = jnp.zeros_like(grad_scores)
    grad_cum_t[...] = jnp.zeros_like(grad_cum_t)
    grad_cum_ref[...] = cum_in_ref[...]
    lanes = lax.broadcasted_iota(jnp.int32, (1, LANES), 1)

    def pair(index, carry):
        chunk = pl.ds(pl.multiple_of(index * LANES, LANES), LANES)
        values = conv_ref[:, chunk]
        delta = wide_delta[:, chunk]
        scaled = values * delta
        columns = wide_cum[:, chunk]
        grad_out = grad_ssd_ref[:, chunk]
        grad_scaled = jnp.zeros_like(scaled)
        scaled = bf16_terms(scaled, 2)
        grad_terms = bf16_terms(grad_out, 2)
        for half in range(PAIR):
            head = index * PAIR + half
            column = columns[:, half * HEAD_DIM : half * HEAD_DIM + 1]
            row = cum_t[pl.ds(head, 1), :]
            kernel = jnp.exp((column - row) * allowed[...]) * allowed[...]
            mixing = kernel * scores[...]
            part = [term * head_half(half).astype(jnp.bfloat16) for term in grad_terms]
            grad_scaled = grad_scaled + terms_dot(bf16_terms(mixing, 2), part, ((0,), (0,)), 2)
            grad_mixing = terms_dot(part, scaled, ((1,), (1,)), 2)
            grad_scores[...] += grad_mixing * kernel
            grad_gap = grad_mixing * mixing
            later = jnp.sum(grad_gap, axis=1, keepdims=True)
            grad_cum_ref[...] += jnp.where(lanes == head, later, 0.0)
            grad_cum_t[pl.ds(head, 1), :] = jnp.sum(grad_gap, axis=0, keepdims=True)
        grad_values_ref[:, chunk] = grad_scaled * delta + grad_out * skip_ref[:, chunk]
        by_delta[:, chunk] = grad_scaled * values
        grad_skip_ref[:, chunk] = jnp.sum(grad_out * values, axis=0, keepdims=True)
        return carry

    lax.fori_loop(0, PAIRS, pair, 0)
    grad_cum_ref[...] -= grad_cum_t[...].T
    grad_delta_ref[...] = gather_heads(by_delta[...])
    grad_reads_ref[...] = reads_in_ref[...] + exact_dot(grad_scores[...], writes)
    grad_writes_ref[...] = exact_dot(grad_scores[...], reads, ((0,), (0,)))


def conv_grad_kernel(
    after_ref, state_ref, grad_values_ref, grad_writes_ref, grad_reads_ref, grad_cum_ref, grad_delta_ref,
    conv_ref, ext_ref, same_ref, weight_ref, bias_ref, delta_ref, cum_ref, seg_ref, prev_ref,
    dt_ref, dt_bias_ref, a_log_ref,
    grad_ext_ref, grad_weight_ref, grad_bias_ref, grad_dt_ref, grad_a_log_ref, grad_dt_bias_ref,
    grad_conv, from_state_ref,
):
    length = delta_ref.shape[0]
    last = length - 1
    writes = conv_ref[:, INNER : INNER + STATE]
    values = conv_ref[:, :INNER]
    delta = delta_ref[...]
    cum = cum_ref[...]
    shrink = end_scale(cum, seg_ref[...])
    end_weight = spread(shrink * delta)
    from_state_ref[...] = exact_dot(writes, after_ref[...], ((1,), (1,)))
    grad_conv[:, :INNER] = grad_values_ref[...] + from_state_ref[...] * end_weight
    grad_conv[:, INNER : INNER + STATE] = grad_writes_ref[...] + exact_dot(
        values * end_weight, after_ref[...]
    )
    grad_conv[:, INNER + STATE :] = grad_reads_ref[...]
    grad_end = gather_heads(from_state_ref[...] * values)
    grad_delta = grad_delta_ref[...] + grad_end * shrink
    moved = grad_end * (shrink * delta)
    per_channel = jnp.sum(state_ref[...] * after_ref[...], axis=1, keepdims=True)
    kept = jnp.sum(per_channel * head_of_channel(True).astype(jnp.float32), axis=0, keepdims=True)
    linked = linked_rows(seg_ref[...], prev_ref)
    grad_last = jnp.sum(moved, axis=0, keepdims=True) + (
        jnp.exp(cum[last:, :]) * linked[last:, :] * kept
    )
    row = lax.broadcasted_iota(jnp.int32, (length, 1), 0)
    grad_cum = grad_cum_ref[...] - moved + jnp.where(row == last, grad_last, 0.0)
    since = ordered(length, True).astype(jnp.bfloat16)
    grad_decay = terms_dot([since], bf16_terms(grad_cum, 3), ((1,), (0,)), 3)
    rate = jnp.exp(a_log_ref[...])
    grad_a_log_ref[...] = jnp.sum(-grad_decay * delta * rate, axis=0, keepdims=True)
    grad_dt = (grad_delta - grad_decay * rate) * sigmoid(dt_ref[...] + dt_bias_ref[...])
    grad_dt_ref[...] = grad_dt
    grad_dt_bias_ref[...] = jnp.sum(grad_dt, axis=0, keepdims=True)
    before = conv_before(ext_ref, same_ref, weight_ref, bias_ref)
    opened = sigmoid(before)
    grad_before = grad_conv[...] * (opened * (1.0 + before * (1.0 - opened)))
    grad_bias_ref[...] = jnp.sum(grad_before, axis=0, keepdims=True)
    grad_ext_ref[...] = jnp.zeros_like(grad_ext_ref)
    grad_weight_ref[...] = jnp.zeros_like(grad_weight_ref)
    for tap in range(CONV_WIDTH):
        place = pl.ds(SUBLANES - (CONV_WIDTH - 1) + tap, length)
        reached = grad_before * same_ref[:, tap : tap + 1]
        grad_weight_ref[tap : tap + 1, :] = jnp.sum(
            reached * ext_ref[place, :], axis=0, keepdims=True
        )
        grad_ext_ref[place, :] += reached * weight_ref[tap : tap + 1, :]


def local_call(kernel, shapes, scratch, name, flops, *args):
    spaces = [
        pl.BlockSpec(memory_space=pltpu.SMEM if arg.dtype == jnp.int32 and arg.ndim == 1 else pltpu.VMEM)
        for arg in args
    ]
    return pl.pallas_call(
        kernel,
        out_shape=[jax.ShapeDtypeStruct(*shape) for shape in shapes],
        in_specs=spaces,
        out_specs=[pl.BlockSpec(memory_space=pltpu.VMEM)] * len(shapes),
        scratch_shapes=[pltpu.VMEM(*shape) for shape in scratch],
        compiler_params=pltpu.CompilerParams(vmem_limit_bytes=VMEM_LIMIT),
        cost_estimate=pl.CostEstimate(
            flops=flops, bytes_accessed=sum(a.size * a.dtype.itemsize for a in args), transcendentals=0
        ),
        name=name,
    )(*args)


def f32(*shape):
    return (shape, jnp.float32)


def bf16(*shape):
    return (shape, jnp.bfloat16)


def pad_heads(array):
    return jnp.pad(array, [(0, 0)] * (array.ndim - 1) + [(0, LANES - HEADS)])


def on_device(tokens, cotangent, segments, params, first_moment, second_moment):
    length = tokens.shape[0]
    lag_rows = CONV_WIDTH - 1
    gathered = gather_params(params)
    picks = fold_picks()
    tail_tok, tail_seg = shifted((tokens[length - lag_rows :], segments[length - lag_rows :]), "grp", 1)
    ext_tok = jnp.concatenate(
        [jnp.zeros((ROW_ALIGN - lag_rows, D), tokens.dtype), tail_tok, tokens], 0
    )
    tok_f = jnp.dot(ext_tok, picks, preferred_element_type=jnp.float32)
    inverse = lax.rsqrt(jnp.mean(tok_f * tok_f, axis=-1, keepdims=True) + EPSILON)
    normed = tok_f * inverse
    w_in, w_out, conv_w, conv_b, norm_gain, gate_gain, dt_bias, a_log, d_skip = unpack_weights(gathered)
    conv_w_f = jnp.pad(conv_w.astype(jnp.float32), ((0, SUBLANES - CONV_WIDTH), (0, 0)))
    conv_b_f = conv_b.astype(jnp.float32)[None]
    gate_gain_f = gate_gain.astype(jnp.float32)[None]
    dt_bias_f = pad_heads(dt_bias.astype(jnp.float32)[None])
    a_log_f = pad_heads(a_log.astype(jnp.float32)[None])
    d_skip_f = jnp.repeat(d_skip.astype(jnp.float32), HEAD_DIM)[None]
    norm_f = norm_gain.astype(jnp.float32).reshape(FOLD_ROWS, FOLD).T.reshape(-1)
    hidden_in = (normed * norm_f).astype(jnp.bfloat16)
    projected = jnp.dot(hidden_in, w_in, preferred_element_type=jnp.float32).astype(jnp.bfloat16)
    hidden_in, normed, inverse = hidden_in[ROW_ALIGN:], normed[ROW_ALIGN:], inverse[ROW_ALIGN:]
    gate_in = projected[ROW_ALIGN:, :INNER]
    extended = projected[ROW_ALIGN - SUBLANES :, INNER : INNER + CONV_CH].astype(jnp.float32)
    dt_raw = pad_heads(projected[ROW_ALIGN:, INNER + CONV_CH :].astype(jnp.float32))
    ext_seg = jnp.concatenate([tail_seg, segments], 0)
    prev_seg = tail_seg[lag_rows - 1 :]
    same = jnp.stack(
        [(ext_seg[tap : tap + length] == segments).astype(jnp.float32) for tap in range(CONV_WIDTH)], 1
    )
    seg_col, seg_row = segments[:, None], segments[None]
    square = f32(length, length)
    unit = length * INNER * STATE * 2
    conv_out, delta, cum, own_state = local_call(
        states_kernel,
        [f32(length, CONV_CH), f32(length, LANES), f32(length, LANES), f32(INNER, STATE)],
        [f32(length, INNER)],
        "states", 20 * unit,
        extended, same, conv_w_f, conv_b_f, dt_raw, dt_bias_f, a_log_f, seg_col,
    )
    linked_last = (segments[length - 1] == prev_seg[0]).astype(jnp.float32)
    through = jnp.exp(cum[length - 1, :HEADS]) * linked_last
    grad_mixed = jnp.dot(cotangent, w_out.T, preferred_element_type=jnp.float32)
    state_in, throughs, grad_mixed = states_before(
        own_state.reshape(HEADS, HEAD_DIM, STATE), through, grad_mixed
    )
    state_in = state_in.reshape(INNER, STATE)
    (own_out,) = local_call(
        inner_kernel,
        [f32(length, INNER)],
        [f32(length, INNER), f32(length, INNER), f32(LANES, length), square, square],
        "inner", 30 * unit,
        conv_out, delta, cum, seg_col, seg_row, d_skip_f,
    )
    mixed_out, grad_ssd, grad_gate_in, own_grad, grad_gate_gain, grad_cum, grad_reads = local_call(
        gate_kernel,
        [
            bf16(length, INNER), f32(length, INNER), bf16(length, INNER), f32(INNER, STATE),
            f32(1, INNER), f32(length, LANES), f32(length, LANES),
        ],
        [f32(length, INNER), f32(length, INNER)],
        "gate", 30 * unit,
        own_out, state_in, conv_out, cum, seg_col, prev_seg, gate_in, grad_mixed, gate_gain_f,
    )
    gate_hidden = jnp.dot(grad_gate_in, w_in[:, :INNER].T, preferred_element_type=jnp.float32)
    grad_state_out, (out_rows, gate_hidden) = grads_after(
        own_grad.reshape(HEADS, HEAD_DIM, STATE),
        throughs,
        (out_grad_rows(mixed_out, cotangent), gate_hidden),
    )
    grad_state_out = grad_state_out.reshape(INNER, STATE)
    activations = (tokens.astype(jnp.float32) + jnp.dot(mixed_out, w_out, preferred_element_type=jnp.float32)).astype(
        jnp.bfloat16
    )
    grad_values, grad_cum, grad_delta, grad_writes, grad_reads, grad_skip = local_call(
        inner_grad_kernel,
        [
            f32(length, INNER), f32(length, LANES), f32(length, LANES), f32(length, STATE),
            f32(length, STATE), f32(1, INNER),
        ],
        [
            f32(length, INNER), f32(length, INNER), f32(LANES, length), square, square, square,
            f32(length, INNER), f32(LANES, length),
        ],
        "inner_grad", 60 * unit,
        grad_ssd, conv_out, delta, cum, seg_col, seg_row, d_skip_f, grad_cum, grad_reads,
    )
    grad_ext, grad_conv_w, grad_conv_b, grad_dtr, grad_a_log, grad_dt_bias = local_call(
        conv_grad_kernel,
        [
            f32(length + SUBLANES, CONV_CH), f32(SUBLANES, CONV_CH), f32(1, CONV_CH),
            f32(length, LANES), f32(1, LANES), f32(1, LANES),
        ],
        [f32(length, CONV_CH), f32(length, INNER)],
        "conv_grad", 30 * unit,
        grad_state_out, state_in, grad_values, grad_writes, grad_reads, grad_cum, grad_delta,
        conv_out, extended, same, conv_w_f, conv_b_f, delta, cum, seg_col, prev_seg,
        dt_raw, dt_bias_f, a_log_f,
    )
    from_next = shifted(grad_ext[SUBLANES - lag_rows : SUBLANES], "grp", -1)
    grad_xbc = grad_ext[SUBLANES:] + jnp.concatenate(
        [jnp.zeros((length - lag_rows, CONV_CH), jnp.float32), from_next], 0
    )
    grad_proj = jnp.concatenate(
        [grad_gate_in, grad_xbc.astype(jnp.bfloat16), grad_dtr[:, :HEADS].astype(jnp.bfloat16)], 1
    )
    grad_hidden = gate_hidden + jnp.dot(
        grad_proj[:, INNER:], w_in[:, INNER:].T, preferred_element_type=jnp.float32
    )
    grad_gain = jnp.sum(grad_hidden * normed, axis=0)
    scaled = grad_hidden * norm_f
    input_grad = cotangent.astype(jnp.float32) + lax.dot_general(
        inverse * (scaled - normed * jnp.mean(scaled * normed, axis=-1, keepdims=True)),
        picks.astype(jnp.float32), (((1,), (1,)), ((), ())), precision=HIGHEST,
    )
    terms = (
        grad_conv_w[:CONV_WIDTH],
        grad_conv_b,
        grad_gain.reshape(FOLD, FOLD_ROWS).T,
        grad_gate_gain,
        grad_dt_bias[:, :HEADS],
        grad_a_log[:, :HEADS],
        jnp.sum(grad_skip.reshape(HEADS, HEAD_DIM), axis=1),
        jnp.zeros((P_TOTAL - P_RAW,), jnp.float32),
    )
    small = jnp.concatenate([term_part.reshape(-1) for term_part in terms]).reshape(-1, LANES)
    grad_shard = sum_grads(
        hidden_in.T.reshape(FOLD, FOLD_ROWS, length), grad_proj, small, out_rows
    )
    new_params, new_first, new_second = adam_update(params, grad_shard, first_moment, second_moment)
    return (activations, input_grad, grad_shard, new_params, new_first, new_second)


def solution(mesh):
    placed = (
        P(("rep", "grp"), None),
        P(("rep", "grp"), None),
        P(("rep", "grp")),
        P("grp"),
        P("grp"),
        P("grp"),
    )
    return jax.shard_map(
        on_device,
        mesh=mesh,
        in_specs=placed,
        out_specs=(
            P(("rep", "grp"), None),
            P(("rep", "grp"), None),
            P("grp"),
            P("grp"),
            P("grp"),
            P("grp"),
        ),
        check_vma=False,
    )
```
